256 devices in a mesh: expert: 32 (over z, y), vocab: 8 (over x, core).
Axes of the slice: x: 4, y: 4, z: 8, core: 2. Of those that a mesh axis runs over, the one named last changes fastest.
Arguments:
- tokens: bfloat16 [8192, 2048], P('expert'), may hold values from -6 to 6
- teacher_expert: int32 [8192, 1], P('expert'), may hold values from 0 to 15
- student_expert: int32 [8192, 1], P('expert'), may hold values from 0 to 15
- priority: int32 [32, 256], P('expert'), may hold values from 0 to 255, each once within a row
- expert_in: bfloat16 [32, 2048, 8192], P('expert', None, 'vocab'), may hold values from -0.125 to 0.125
- expert_out: bfloat16 [32, 8192, 2048], P('expert', 'vocab'), may hold values from -0.0625 to 0.0625
- teacher_gain: float32 [2048], replicated, may hold values from 0.1 to 1.9
- student_gain: float32 [2048], replicated, may hold values from 0.1 to 1.9
- teacher_head: bfloat16 [16384, 2048], P(('vocab', 'expert')), may hold values from -4 to 4
- student_head: bfloat16 [16384, 2048], P(('vocab', 'expert')), may hold values from -4 to 4
Outputs:
- token_kl: float32 [8192], P('expert')
The draws below stay inside these ranges and needn't reach their ends.
Inputs may be any that keep to these rules, and one draw needn't show every extreme that they name: Each row of priority holds every number of 0 to 255 once.
All inputs are finite; a program needn't handle non-finite values.
Results may differ from the reference program's by a relative error of at most 0.0032.
Values may be sent and summed in bfloat16 or wider, within the bound.
A program may use at most 128 MiB of HBM per device.

```python
import math
import jax
import jax.numpy as jnp
from jax import lax

D = 2048
FF = 8192
TOK_DEV = 256
CAP = 24
TOKENS = 8192
VOCAB = 16384
N_EXPERT = 32


def head_matrix(key):
    normal_key, spread_key = jax.random.split(key, 2)
    entries = jax.random.normal(normal_key, (VOCAB, D), jnp.float32)
    vocab_ramp = 1.0 + 2.0 * jnp.arange(VOCAB, dtype=jnp.float32) / VOCAB
    spread = jnp.exp(jax.random.uniform(spread_key, (VOCAB, 1), jnp.float32, math.log(0.3), math.log(3.0)))
    row_scale = spread * vocab_ramp[:, None] / math.sqrt(D)
    matrix = entries * row_scale
    return jnp.clip(matrix, -4.0, 4.0)


def draw_teacher_head(key, part):
    return head_matrix(jax.random.fold_in(key, 101)).astype(jnp.bfloat16)


def draw_student_head(key, part):
    return head_matrix(jax.random.fold_in(key, 202)).astype(jnp.bfloat16)


def steps_of(key, extent, shards, least, top_value):
    def one(dim, blocks):
        steps = jax.random.uniform(jax.random.fold_in(jax.random.fold_in(key, 6), dim), (blocks,), jnp.float32, least / len(shards), top_value / len(shards))
        return jnp.repeat(jnp.exp(steps), extent[dim] // blocks).reshape((-1,) + (1,) * (len(extent) - dim - 1))

    level = one(*shards[0])
    for cut in shards[1:]:
        level = level * one(*cut)
    return level


def picks_of(own_key, rows, number_of, top, lift):
    order = jax.random.permutation(jax.random.fold_in(own_key, 1), number_of)
    pull = order
    for power in range(3):
        pull = pull * pull // number_of
    pull = pull * lift // number_of
    lots = jax.random.randint(jax.random.fold_in(own_key, 2), (rows, number_of), 0, 4096) + pull
    sure = jax.random.permutation(jax.random.fold_in(own_key, 3), rows)[jnp.arange(number_of) % rows]
    lots = jnp.where(jnp.arange(rows)[:, None] == sure[None, :], 1 << 14, lots)
    merit = lots * number_of + jnp.arange(number_of)
    return lax.top_k(merit.astype(jnp.int32), top)[1].astype(jnp.int32)


def gaussian(rng, extent, scale, most, cuts=(), held_as=jnp.bfloat16):
    factor_of = steps_of(rng, extent, cuts, -0.22, 0.18) if cuts else 1.0
    array = jax.random.normal(rng, extent, jnp.float32) * scale * factor_of
    return jnp.minimum(jnp.maximum(array, -most), most).astype(held_as)


def setup_inputs(seed: int = 0) -> dict:
    key_of = jax.random.split(jax.random.key(seed), 11)
    tokens = gaussian(key_of[0], (TOKENS, D), 1.0, 6.0, ((0, 32),))
    teacher_expert = picks_of(key_of[1], TOKENS, N_EXPERT // 2, 1, 512)
    student_expert = picks_of(key_of[2], TOKENS, N_EXPERT // 2, 1, 512)
    priority = jax.vmap(lambda own: jax.random.permutation(own, TOK_DEV))(jax.random.split(key_of[3], N_EXPERT)).reshape((N_EXPERT, TOK_DEV)).astype(jnp.int32)
    expert_in = gaussian(key_of[4], (N_EXPERT, D, FF), D ** -0.5, 0.125, ((0, 32), (2, 8)))
    expert_out = gaussian(key_of[5], (N_EXPERT, FF, D), FF ** -0.5, 0.0625, ((0, 32), (1, 8)))
    teacher_gain = jnp.clip(1.0 + 0.18 * jax.random.normal(key_of[6], (D,), jnp.float32), 0.1, 1.9)
    student_gain = jnp.clip(1.0 + 0.18 * jax.random.normal(key_of[7], (D,), jnp.float32), 0.1, 1.9)
    teacher_head = draw_teacher_head(jax.random.fold_in(key_of[10], 71), 0)
    student_head = draw_student_head(jax.random.fold_in(key_of[10], 71), 0)
    return {"tokens": tokens, "teacher_expert": teacher_expert, "student_expert": student_expert, "priority": priority, "expert_in": expert_in, "expert_out": expert_out, "teacher_gain": teacher_gain, "student_gain": student_gain, "teacher_head": teacher_head, "student_head": student_head}


def slot_places(expert, ranking, capacity, lane, dump):
    same_expert = expert[:, None] == expert[None, :]
    before = ranking[None, :] < ranking[:, None]
    slot_rank = lax.optimization_barrier(jnp.sum(jnp.logical_and(same_expert, before).astype(jnp.int32), axis=1))
    kept_mask = slot_rank < capacity
    return jnp.where(kept_mask, (2 * expert + lane) * capacity + slot_rank, dump).astype(jnp.int32)

def normed(tokens, branch, gain_vector):
    summed = tokens.astype(jnp.float32) + branch.astype(jnp.float32)
    factor = lax.rsqrt(lax.optimization_barrier(jnp.mean(summed * summed, axis=-1, keepdims=True)) + 1e-05)
    return (summed * factor * gain_vector).astype(jnp.bfloat16)

def reference(tokens, teacher_expert, student_expert, priority, expert_in, expert_out, teacher_gain, student_gain, teacher_head, student_head):
    groups = N_EXPERT
    dump = groups * CAP
    blocks = tokens.reshape(groups, TOK_DEV, D)
    teacher_ids = teacher_expert.reshape(groups, TOK_DEV)
    student_ids = student_expert.reshape(groups, TOK_DEV)
    teacher_places = jax.vmap(slot_places, in_axes=(0, 0, None, None, None))(teacher_ids, priority, CAP, 0, dump)
    student_places = jax.vmap(slot_places, in_axes=(0, 0, None, None, None))(student_ids, priority, CAP, 1, dump)
    numbers = jnp.arange(TOK_DEV, dtype=jnp.int32)

    def owners_of(first, second):
        filled = jnp.full((dump + 1,), TOK_DEV, jnp.int32).at[first].set(numbers).at[second].set(numbers)
        return filled[:dump]
    owners = jax.vmap(owners_of)(teacher_places, student_places)
    padded = jnp.concatenate([blocks, jnp.zeros((groups, 1, D), jnp.bfloat16)], axis=1)
    outgoing = jax.vmap(lambda source, picked: source[picked])(padded, owners).reshape(groups, groups, CAP, D)

    def run_expert(index):
        received = outgoing[:, index].reshape(groups * CAP, D)
        hidden = jax.nn.gelu(jnp.dot(received, expert_in[index], preferred_element_type=jnp.float32)).astype(jnp.bfloat16)
        result = jnp.dot(hidden, expert_out[index], preferred_element_type=jnp.float32).astype(jnp.bfloat16)
        return result.reshape(groups, CAP, D)
    results = lax.map(run_expert, jnp.arange(groups, dtype=jnp.int32))
    returned = jnp.transpose(results, (1, 0, 2, 3)).reshape(groups, dump, D)
    returned = jnp.concatenate([returned, jnp.zeros((groups, 1, D), jnp.bfloat16)], axis=1)
    teacher_branch = jax.vmap(lambda source, picked: source[picked])(returned, teacher_places)
    student_branch = jax.vmap(lambda source, picked: source[picked])(returned, student_places)
    teacher_normed = normed(blocks, teacher_branch, teacher_gain)
    student_normed = normed(blocks, student_branch, student_gain)

    def block_loss(paired):
        teacher_rows, student_rows = paired
        teacher_logits = jnp.dot(teacher_rows, teacher_head.T, preferred_element_type=jnp.float32)
        student_logits = jnp.dot(student_rows, student_head.T, preferred_element_type=jnp.float32)
        teacher_log = jax.nn.log_softmax(teacher_logits, axis=-1)
        student_log = jax.nn.log_softmax(student_logits, axis=-1)
        return lax.optimization_barrier(jnp.sum(jnp.exp(teacher_log) * (teacher_log - student_log), axis=-1))
    return lax.map(block_loss, (teacher_normed, student_normed)).reshape(TOKENS)
```

```python
import jax
import jax.numpy as jnp
from jax import lax
from jax.experimental import pallas as pl
from jax.experimental.pallas import tpu as pltpu
from jax.sharding import PartitionSpec as P

MESH = pl.DeviceIdType.MESH
BF = jnp.bfloat16
F32 = jnp.float32
CAP = 24
NT = (((1,), (1,)), ((), ()))


def gelu(v):
    return 0.5 * v * (1.0 + jnp.tanh(0.7978845608028654 * (v + 0.044715 * v * v * v)))


def kernel(
    tok_hbm, te_ref, se_ref, pr_ref, win_hbm, wout_hbm, tg_ref, sg_ref, th_hbm, sh_hbm,
    o_ref,
    tok, out_rows, feats, w1, w2, acc, hid, part_send, part_recv, own_part,
    back, ret, unit, units, heads, st_send, st_recv, pick,
    load_sem, w_send, w_recv, disp_send, disp_recv, xag_send, xag_recv,
    rs_send, rs_recv, comb_send, comb_recv, pair_send, pair_recv,
    ag_send, ag_recv, hd_send, hd_recv, hp_send, hp_recv, st_ssem, st_rsem,
):
    e = lax.axis_index("expert")
    v = lax.axis_index("vocab")
    z, y = e // 4, e % 4
    x, c = v // 2, v % 2
    mate = 1 - c
    home = e // 16

    def at(zz, yy, xx, cc):
        return (zz * 4 + yy, xx * 2 + cc)

    def step(a, d, n):
        return lax.rem(a + d + n, n)

    xr, xl, xo = step(x, 1, 4), step(x, -1, 4), step(x, 2, 4)

    def remote(src, dst, ssem, rsem, dev):
        return pltpu.make_async_remote_copy(
            src_ref=src, dst_ref=dst, send_sem=ssem, recv_sem=rsem,
            device_id=dev, device_id_type=MESH,
        )

    cp_tok = pltpu.make_async_copy(
        tok_hbm.at[:, pl.ds(pl.multiple_of(v * 256, 256), 256)], tok, load_sem.at[0]
    )
    cp_tok.start()
    cp_w1 = pltpu.make_async_copy(win_hbm.at[0], w1.at[c], load_sem.at[1])
    cp_w2 = pltpu.make_async_copy(wout_hbm.at[0], w2.at[c], load_sem.at[2])
    cp_th = pltpu.make_async_copy(th_hbm, heads.at[z, c, 0], load_sem.at[3])
    cp_sh = pltpu.make_async_copy(sh_hbm, heads.at[z, c, 1], load_sem.at[4])
    rw1 = remote(win_hbm.at[0], w1.at[c], w_send.at[0], w_recv.at[0], at(z, y, x, mate))
    rw2 = remote(wout_hbm.at[0], w2.at[c], w_send.at[1], w_recv.at[1], at(z, y, x, mate))
    rw1.start()
    cp_w1.start()

    def spread(row):
        return jnp.broadcast_to(row.astype(F32), (256, 256))

    pj = spread(pr_ref[...])
    pi = pj.T

    def places(expert_ref, lane):
        ej = spread(expert_ref[...])
        ei = ej.T
        same = ei == ej
        rank_row = jnp.sum(jnp.where(same & (pi < pj), 1.0, 0.0), axis=0, keepdims=True)
        rank_col = jnp.sum(jnp.where(same & (pj < pi), 1.0, 0.0), axis=1, keepdims=True)

        def place(expert, rank):
            return jnp.where(rank < CAP, (2.0 * expert + lane) * CAP + rank, -1.0)

        return place(ej[:1], rank_row), place(ei[:, :1], rank_col)

    t_row, t_col = places(te_ref, 0.0)
    s_row, s_col = places(se_ref, 1.0)
    slot = lax.broadcasted_iota(jnp.int32, (768, 256), 0).astype(F32)
    gather = jnp.where((slot == t_row) | (slot == s_row), 1.0, 0.0).astype(BF)
    lanes = lax.broadcasted_iota(jnp.int32, (256, 768), 1).astype(F32)
    pick[0:256] = jnp.where(lanes == t_col, 1.0, 0.0).astype(BF)
    pick[256:512] = jnp.where(lanes == s_col, 1.0, 0.0).astype(BF)
    cp_tok.wait()
    picked = jnp.dot(gather, tok[...], preferred_element_type=F32)
    out_rows[...] = picked.reshape(96, 8, 256).astype(BF)

    my_slot = pl.ds(3 * lax.rem(e, 16), 3)

    def disp(to):
        return remote(
            out_rows.at[pl.ds(3 * to, 3)], feats.at[x, c, my_slot],
            disp_send.at[to], disp_recv.at[lax.rem(e, 16), c], (to, x * 2 + home),
        )

    cp_self = pltpu.make_async_copy(
        out_rows.at[pl.ds(3 * e, 3)], feats.at[x, c, my_slot], load_sem.at[5]
    )

    @pl.when(home == c)
    def _():
        cp_self.start()

    @pl.when(home != c)
    def _():
        disp(e).start()

    def send_rows(r, carry):
        disp(lax.rem(e + r, 32)).start()
        return carry

    lax.fori_loop(1, 32, send_rows, 0)
    rw2.start()
    cp_w2.start()
    cp_th.start()
    cp_sh.start()

    def arrived_rows(cc, j):
        here = feats.at[x, cc, pl.ds(3 * j, 3)]
        return remote(
            here, here, disp_send.at[0], disp_recv.at[j, cc], at(z, y, x, mate)
        )

    def wait_rows(cc):
        def wait_one(j, carry):
            @pl.when(jnp.logical_not((c * 16 + j == e) & (cc == c)))
            def _():
                arrived_rows(cc, j).wait_recv()

            return carry

        lax.fori_loop(0, 16, wait_one, 0)

    @pl.when(home == c)
    def _():
        cp_self.wait()

    def xcopy(xx, cc, k, to):
        piece = feats.at[xx, cc]
        return remote(piece, piece, xag_send.at[k], xag_recv.at[k], at(z, y, to, c))

    wait_rows(0)
    xcopy(x, 0, 0, xr).start()
    wait_rows(1)
    xcopy(x, 1, 1, xl).start()
    xcopy(x, 1, 2, xr).start()
    xcopy(x, 0, 3, xl).start()

    zu, zd = step(z, 1, 8), step(z, -1, 8)
    cp_th.wait()
    cp_sh.wait()

    def ring_up(zz, k, both):
        piece = heads.at[zz, c] if both else heads.at[zz, c, 0]
        return remote(piece, piece, hd_send.at[0, k], hd_recv.at[0, k], at(zu, y, x, c))

    def ring_down(zz, k, both):
        piece = heads.at[zz, c] if both else heads.at[zz, c, 1]
        return remote(piece, piece, hd_send.at[1, k], hd_recv.at[1, k], at(zd, y, x, c))

    def to_mate(zz, cc, k):
        piece = heads.at[zz, cc]
        return remote(piece, piece, hp_send.at[k], hp_recv.at[k], at(z, y, x, mate))

    ring_up(z, 0, True).start()
    ring_down(z, 0, True).start()
    to_mate(z, c, 0).start()

    cp_w1.wait()
    rw1.wait_recv()

    def rows_of(xx):
        return [
            feats[xx, cc].astype(F32).reshape(384, 256).astype(BF) for cc in (0, 1)
        ]

    def hidden_pass(xs, first, last):
        for cc in (0, 1):
            def body(n, carry):
                cols = pl.ds(pl.multiple_of(n * 256, 256), 256)
                total = None if first else acc[cc, :, cols]
                for xx in xs:
                    left = jnp.concatenate(rows_of(xx), axis=1)
                    k = pl.ds(pl.multiple_of(xx * 512, 512), 512)
                    term = jnp.dot(left, w1[cc, k, cols], preferred_element_type=F32)
                    total = term if total is None else total + term
                if last:
                    hid[cc, :, cols] = gelu(total).astype(BF)
                else:
                    acc[cc, :, cols] = total
                return carry

            lax.fori_loop(0, 4, body, 0)

    hidden_pass([x], True, False)
    xcopy(xl, 0, 0, xr).wait_recv()
    xcopy(xl, 0, 4, xr).start()
    xcopy(xr, 1, 1, xl).wait_recv()
    xcopy(xr, 1, 5, xl).start()
    xcopy(xl, 1, 2, xr).wait_recv()
    xcopy(xr, 0, 3, xl).wait_recv()
    hidden_pass([xl, xr], False, False)
    xcopy(xo, 0, 4, xr).wait_recv()
    xcopy(xo, 1, 5, xl).wait_recv()

    def ring_next(k):
        lo, hi = step(z, -k, 8), step(z, k, 8)
        ring_up(lo, k - 1, True).wait_recv()
        ring_down(hi, k - 1, True).wait_recv()
        ring_up(lo, k, k < 3).start()
        ring_down(hi, k, k < 3).start()
        to_mate(lo, c, 2 * k - 1).start()
        to_mate(hi, c, 2 * k).start()

    ring_next(1)
    hidden_pass([xo], False, True)

    cp_w2.wait()
    rw2.wait_recv()

    def partial(xx, half):
        cols = pl.ds(pl.multiple_of(xx * 512 + half * 256, 256), 256)
        return jnp.dot(hid[0], w2[0, :, cols], preferred_element_type=F32) + jnp.dot(
            hid[1], w2[1, :, cols], preferred_element_type=F32
        )

    def rs(k, to):
        return remote(
            part_send.at[k], part_recv.at[k], rs_send.at[k], rs_recv.at[k], at(z, y, to, c)
        )

    part_send[0] = partial(xo, 0).astype(BF)
    rs(0, xr).start()
    part_send[1] = partial(xo, 1).astype(BF)
    rs(1, xl).start()
    part_send[2] = partial(xr, 1).astype(BF)
    rs(2, xr).start()
    part_send[3] = partial(xl, 0).astype(BF)
    rs(3, xl).start()
    mine = partial(xr, 0)
    rs(0, xr).wait_recv()
    part_send[4] = (mine + part_recv[0].astype(F32)).astype(BF)
    rs(4, xr).start()
    mine = partial(xl, 1)
    rs(1, xl).wait_recv()
    part_send[5] = (mine + part_recv[1].astype(F32)).astype(BF)
    rs(5, xl).start()
    own_part[0] = partial(x, 0)
    own_part[1] = partial(x, 1)
    ring_next(2)
    rs(2, xr).wait_recv()
    rs(3, xl).wait_recv()

    def comb(b, cc):
        return remote(
            back.at[cc, pl.ds(3 * lax.rem(b, 16), 3)], ret.at[pl.ds(3 * e, 3)],
            comb_send.at[cc, lax.rem(b, 16)], comb_recv.at[e], (b, x * 2 + cc),
        )

    def send_back(cc):
        def one(r, carry):
            b = c * 16 + lax.rem(e + r, 16)

            @pl.when(jnp.logical_not((b == e) & (cc == c)))
            def _():
                comb(b, cc).start()

            return carry

        lax.fori_loop(0, 16, one, 0)

    rs(4, xr).wait_recv()
    total = own_part[0] + part_recv[3].astype(F32) + part_recv[4].astype(F32)
    back[0] = total.reshape(48, 8, 256).astype(BF)
    send_back(0)
    rs(5, xl).wait_recv()
    total = own_part[1] + part_recv[2].astype(F32) + part_recv[5].astype(F32)
    back[1] = total.reshape(48, 8, 256).astype(BF)
    send_back(1)
    cp_back = pltpu.make_async_copy(
        back.at[c, pl.ds(3 * lax.rem(e, 16), 3)], ret.at[pl.ds(3 * e, 3)], load_sem.at[6]
    )

    @pl.when(home == c)
    def _():
        cp_back.start()
        cp_back.wait()

    def wait_back(r, carry):
        @pl.when(jnp.logical_not((r == e) & (home == c)))
        def _():
            here = ret.at[pl.ds(3 * r, 3)]
            remote(
                here, here, comb_send.at[0, 0], comb_recv.at[r], at(z, y, x, mate)
            ).wait_recv()

        return carry

    lax.fori_loop(0, 32, wait_back, 0)
    ring_next(3)

    rows = ret[...].astype(F32).reshape(768, 256).astype(BF)
    stream = tok[...].astype(F32)
    squares = []
    cols = pl.ds(pl.multiple_of(v * 256, 256), 256)
    for k, gain_ref in enumerate((tg_ref, sg_ref)):
        branch = jnp.dot(
            pick[256 * k : 256 * k + 256], rows, preferred_element_type=F32
        )
        summed = stream + branch
        scaled = (summed * gain_ref[:, cols]).astype(BF)
        unit[0, 128 * k : 128 * k + 128] = scaled[:128]
        unit[1, 128 * k : 128 * k + 128] = scaled[128:]
        column = jnp.sum(summed * summed, axis=1, keepdims=True)
        squares.append(jnp.broadcast_to(column, (256, 128)).T[:1])
    low = lax.broadcasted_iota(jnp.int32, (16, 256), 0) == 0
    for h in (0, 1):
        lines = []
        for k in (0, 1):
            part = squares[k][:, 128 * h : 128 * h + 128]
            top = part.astype(BF).astype(F32)
            lines.append(
                jnp.broadcast_to(jnp.concatenate([top, part - top], axis=1), (16, 256))
            )
        unit[h, 256:272] = jnp.where(low, lines[0], lines[1]).astype(BF)
    swap = remote(
        unit.at[mate], units.at[y, x, c], pair_send.at[0], pair_recv.at[0], at(z, y, x, mate)
    )
    swap.start()
    cp_unit = pltpu.make_async_copy(unit.at[c], units.at[y, x, c], load_sem.at[7])
    cp_unit.start()
    cp_unit.wait()
    remote(
        unit.at[mate], units.at[y, x, mate], pair_send.at[0], pair_recv.at[0],
        at(z, y, x, mate),
    ).wait_recv()

    here = (x, y)

    def place_of(axis, a, b):
        return units.at[b, a, 0] if axis == 0 else units.at[a, b, 1]

    def dev_of(axis, d):
        p, q = (step(x, d, 4), y) if axis == 0 else (x, step(y, d, 4))
        return at(z, q, p, c)

    def hop(axis, along, a, b, k, d, rows_=None):
        piece = place_of(axis, a, b)
        if rows_ is not None:
            piece = piece.at[rows_[0] : rows_[1]]
        return remote(piece, piece, ag_send.at[axis, k], ag_recv.at[axis, k], dev_of(along, d))

    halves = ((0, 128), (128, 272))

    def first(axis, k, off, d, rows_=None):
        a = step(here[axis], off, 4)
        return hop(axis, axis, a, here[1 - axis], k, d, rows_)

    def second(axis, rel, off, kind, d):
        a = step(here[axis], rel, 4)
        b = step(here[1 - axis], off, 4)
        return hop(axis, 1 - axis, a, b, 4 + 3 * rel + kind, d)

    both = (0, 1)
    for axis in both:
        first(axis, 0, 0, 1).start()
        first(axis, 1, 0, -1).start()
    for axis in both:
        second(axis, 0, 0, 0, 1).start()
        second(axis, 0, 0, 1, -1).start()
    for axis in both:
        first(axis, 0, -1, 1).wait_recv()
        first(axis, 2, -1, 1, halves[0]).start()
        first(axis, 1, 1, -1).wait_recv()
        first(axis, 3, 1, -1, halves[1]).start()
    for axis in both:
        for rel in (3, 1):
            second(axis, rel, 0, 0, 1).start()
            second(axis, rel, 0, 1, -1).start()
    for axis in both:
        first(axis, 2, 2, 1, halves[0]).wait_recv()
        first(axis, 3, 2, -1, halves[1]).wait_recv()
        second(axis, 2, 0, 0, 1).start()
        second(axis, 2, 0, 1, -1).start()
    for rel in (0, 3, 1, 2):
        for axis in both:
            second(axis, rel, -1, 0, 1).wait_recv()
            second(axis, rel, 1, 1, -1).wait_recv()
            if rel in (0, 1):
                second(axis, rel, -1, 2, 1).start()
            else:
                second(axis, rel, 1, 2, -1).start()
    ring_up(step(z, 4, 8), 3, False).wait_recv()
    ring_down(step(z, 4, 8), 3, False).wait_recv()
    to_mate(step(z, 4, 8), c, 7).start()
    for k in range(8):
        off = 0 if k == 0 else (4 if k == 7 else ((k + 1) // 2) * (-1 if k % 2 else 1))
        to_mate(step(z, off, 8), mate, k).wait_recv()
    for rel in (0, 3, 1, 2):
        for axis in both:
            second(axis, rel, 2, 2, 1 if rel in (0, 1) else -1).wait_recv()

    for pair in (0, 1):
        scales = []
        for k in (0, 1):
            parts = []
            for yy in (2 * pair, 2 * pair + 1):
                total = jnp.zeros((1, 128), F32)
                for xx in range(4):
                    for cc in (0, 1):
                        line = units[yy, xx, cc, 256:272, :].astype(F32)[k : k + 1]
                        total = total + line[:, :128] + line[:, 128:]
                parts.append(lax.rsqrt(total * (1.0 / 2048.0) + 1e-5))
            scales.append(jnp.concatenate(parts, axis=1))

        def logits(k, zz):
            left = heads[pl.ds(zz, 4), :, k].reshape(512, 2048)
            total = None
            for xx in range(4):
                for cc in (0, 1):
                    right = jnp.concatenate(
                        [
                            units[2 * pair + i, xx, cc, 128 * k : 128 * k + 128, :]
                            for i in (0, 1)
                        ],
                        axis=0,
                    )
                    kk = (xx * 2 + cc) * 256
                    term = lax.dot_general(
                        left[:, kk : kk + 256], right, NT, preferred_element_type=F32
                    )
                    total = term if total is None else total + term
            return total * scales[k]

        def chunk(n, carry):
            tm, ts, tw, sm, ss = carry
            tl = logits(0, 4 * n)
            sl = logits(1, 4 * n)
            tm2 = jnp.maximum(tm, jnp.max(tl, axis=0, keepdims=True))
            sm2 = jnp.maximum(sm, jnp.max(sl, axis=0, keepdims=True))
            te = jnp.exp(tl - tm2)
            keep = jnp.exp(tm - tm2)
            ts2 = ts * keep + jnp.sum(te, axis=0, keepdims=True)
            tw2 = tw * keep + jnp.sum(te * (tl - sl), axis=0, keepdims=True)
            ss2 = ss * jnp.exp(sm - sm2) + jnp.sum(jnp.exp(sl - sm2), axis=0, keepdims=True)
            return tm2, ts2, tw2, sm2, ss2

        low_row = jnp.full((1, 256), -1e30, F32)
        zero = jnp.zeros((1, 256), F32)
        stats = lax.fori_loop(0, 2, chunk, (low_row, zero, zero, low_row, zero))
        table = jnp.concatenate(list(stats) + [zero, zero, zero], axis=0)
        st_send[2 * pair] = table[:, :128]
        st_send[2 * pair + 1] = table[:, 128:]

    me = 4 * y + x

    def st_copy(r):
        yy = lax.rem(y + r // 8, 4)
        vv = lax.rem(v + lax.rem(r, 8), 8)
        return remote(
            st_send.at[yy], st_recv.at[c, me], st_ssem.at[r], st_rsem.at[c, me],
            (z * 4 + yy, vv),
        )

    def send_stats(r, carry):
        st_copy(r).start()
        return carry

    lax.fori_loop(1, 32, send_stats, 0)
    cp_st = pltpu.make_async_copy(st_send.at[y], st_recv.at[c, me], load_sem.at[8])
    cp_st.start()
    cp_st.wait()

    def wait_stats(r, carry):
        cc, k = r // 16, lax.rem(r, 16)

        @pl.when(jnp.logical_not((cc == c) & (k == me)))
        def _():
            remote(
                st_send.at[0], st_recv.at[cc, k], st_ssem.at[0], st_rsem.at[cc, k],
                at(z, y, x, mate),
            ).wait_recv()

        return carry

    lax.fori_loop(0, 32, wait_stats, 0)
    for cc in (0, 1):
        pieces = st_recv[cc]
        tm, sm = pieces[:, 0], pieces[:, 3]
        tmax = jnp.max(tm, axis=0, keepdims=True)
        smax = jnp.max(sm, axis=0, keepdims=True)
        tk, sk = jnp.exp(tm - tmax), jnp.exp(sm - smax)
        ts = jnp.sum(pieces[:, 1] * tk, axis=0, keepdims=True)
        tw = jnp.sum(pieces[:, 2] * tk, axis=0, keepdims=True)
        ss = jnp.sum(pieces[:, 4] * sk, axis=0, keepdims=True)
        o_ref[cc : cc + 1, :] = tw / ts - tmax - jnp.log(ts) + smax + jnp.log(ss)

    rw1.wait_send()
    rw2.wait_send()

    @pl.when(home != c)
    def _():
        disp(e).wait_send()

    def sent_rows(r, carry):
        disp(lax.rem(e + r, 32)).wait_send()
        return carry

    lax.fori_loop(1, 32, sent_rows, 0)
    for k in range(6):
        xcopy(x, 0, k, xr).wait_send()
        rs(k, xr).wait_send()

    def sent_back(r, carry):
        for cc in (0, 1):
            b = c * 16 + lax.rem(e + r, 16)

            @pl.when(jnp.logical_not((b == e) & (cc == c)))
            def _():
                comb(b, cc).wait_send()

        return carry

    lax.fori_loop(0, 16, sent_back, 0)
    swap.wait_send()
    for axis in both:
        first(axis, 0, 0, 1).wait_send()
        first(axis, 1, 0, -1).wait_send()
        first(axis, 2, -1, 1, halves[0]).wait_send()
        first(axis, 3, 1, -1, halves[1]).wait_send()
        for k in range(4, 16):
            hop(axis, axis, x, y, k, 1).wait_send()
    for k in range(4):
        ring_up(z, k, k < 3).wait_send()
        ring_down(z, k, k < 3).wait_send()
    for k in range(8):
        to_mate(z, c, k).wait_send()

    def sent_stats(r, carry):
        st_copy(r).wait_send()
        return carry

    lax.fori_loop(1, 32, sent_stats, 0)


def local(
    tokens, teacher_expert, student_expert, priority, expert_in, expert_out,
    teacher_gain, student_gain, teacher_head, student_head,
):
    dma = pltpu.SemaphoreType.DMA
    vm = pltpu.VMEM
    whole = pl.BlockSpec(memory_space=pltpu.VMEM)
    out = pl.pallas_call(
        kernel,
        out_shape=jax.ShapeDtypeStruct((2, 128), F32),
        in_specs=[
            pl.BlockSpec(memory_space=pl.ANY), whole, whole, whole,
            pl.BlockSpec(memory_space=pl.ANY), pl.BlockSpec(memory_space=pl.ANY),
            whole, whole,
            pl.BlockSpec(memory_space=pl.ANY), pl.BlockSpec(memory_space=pl.ANY),
        ],
        out_specs=whole,
        scratch_shapes=[
            vm((256, 256), BF),
            vm((96, 8, 256), BF),
            vm((4, 2, 48, 8, 256), BF),
            vm((2, 2048, 1024), BF),
            vm((2, 1024, 2048), BF),
            vm((2, 384, 1024), F32),
            vm((2, 384, 1024), BF),
            vm((6, 384, 256), BF),
            vm((6, 384, 256), BF),
            vm((2, 384, 256), F32),
            vm((2, 48, 8, 256), BF),
            vm((96, 8, 256), BF),
            vm((2, 272, 256), BF),
            vm((4, 4, 2, 272, 256), BF),
            vm((8, 2, 2, 64, 2048), BF),
            vm((4, 8, 128), F32),
            vm((2, 16, 8, 128), F32),
            vm((512, 768), BF),
            dma((9,)),
            dma((2,)), dma((2,)),
            dma((32,)), dma((16, 2)),
            dma((6,)), dma((6,)),
            dma((6,)), dma((6,)),
            dma((2, 16)), dma((32,)),
            dma((1,)), dma((1,)),
            dma((2, 16)), dma((2, 16)),
            dma((2, 4)), dma((2, 4)),
            dma((8,)), dma((8,)),
            dma((32,)), dma((2, 16)),
        ],
        compiler_params=pltpu.CompilerParams(
            has_side_effects=True, vmem_limit_bytes=64 * 1024 * 1024 - 65536
        ),
    )(
        tokens,
        teacher_expert.reshape(1, -1),
        student_expert.reshape(1, -1),
        priority,
        expert_in,
        expert_out,
        teacher_gain.reshape(1, -1),
        student_gain.reshape(1, -1),
        teacher_head,
        student_head,
    )
    return out.reshape(256)


def solution(mesh):
    placed = (
        P("expert", None),
        P("expert", None),
        P("expert", None),
        P("expert", None),
        P("expert", None, "vocab"),
        P("expert", "vocab", None),
        P(),
        P(),
        P(("vocab", "expert"), None),
        P(("vocab", "expert"), None),
    )
    return jax.shard_map(local, mesh=mesh, in_specs=placed, out_specs=P("expert"), check_vma=False)
```

```python
import jax
import jax.numpy as jnp
from jax import lax
from jax.experimental import pallas as pl
from jax.experimental.pallas import tpu as pltpu
from jax.sharding import PartitionSpec as P

MESH = pl.DeviceIdType.MESH
BF = jnp.bfloat16
F32 = jnp.float32
CAP = 24
NT = (((1,), (1,)), ((), ()))


def gelu(v):
    return 0.5 * v * (1.0 + jnp.tanh(0.7978845608028654 * (v + 0.044715 * v * v * v)))


def kernel(
    tok_hbm, te_ref, se_ref, pr_ref, win_hbm, wout_hbm, tg_ref, sg_ref, th_hbm, sh_hbm,
    o_ref,
    tok, out_rows, feats, w1, w2, acc, hid, part_send, part_recv, own_part, xin,
    back, ret, unit, units, heads, st_send, st_recv, pick,
    load_sem, w_send, w_recv, disp_send, disp_recv, xag_send, xag_recv,
    rs_send, rs_recv, comb_send, comb_recv, pair_send, pair_recv,
    ag_send, ag_recv, hd_send, hd_recv, hp_send, hp_recv, st_ssem, st_rsem,
):
    e = lax.axis_index("expert")
    v = lax.axis_index("vocab")
    z, y = e // 4, e % 4
    x, c = v // 2, v % 2
    mate = 1 - c
    home = e // 16

    def at(zz, yy, xx, cc):
        return (zz * 4 + yy, xx * 2 + cc)

    def step(a, d, n):
        return lax.rem(a + d + n, n)

    xr, xl, xo = step(x, 1, 4), step(x, -1, 4), step(x, 2, 4)

    def remote(src, dst, ssem, rsem, dev):
        return pltpu.make_async_remote_copy(
            src_ref=src, dst_ref=dst, send_sem=ssem, recv_sem=rsem,
            device_id=dev, device_id_type=MESH,
        )

    barrier = pltpu.get_barrier_semaphore()

    def greet(ee, vv):
        @pl.when(jnp.logical_not((ee == e) & (vv == v)))
        def _():
            pl.semaphore_signal(barrier, inc=1, device_id=(ee, vv), device_id_type=MESH)

    def greet_rows(r, carry):
        far = lax.rem(e + 16 + r, 32)
        greet(far, x * 2 + home)
        greet(c * 16 + lax.rem(e + r, 16), x * 2 + r // 16)
        greet(z * 4 + r // 8, lax.rem(r, 8))
        return carry

    lax.fori_loop(0, 32, greet_rows, 0)
    greet(step(z, 1, 8) * 4 + y, v)
    greet(step(z, -1, 8) * 4 + y, v)

    cp_tok = pltpu.make_async_copy(
        tok_hbm.at[:, pl.ds(pl.multiple_of(v * 256, 256), 256)], tok, load_sem.at[0]
    )
    cp_tok.start()
    mine_w2 = pl.ds(pl.multiple_of(c * 1024, 1024), 1024)
    cp_w1 = pltpu.make_async_copy(win_hbm.at[0], w1.at[c], load_sem.at[1])
    cp_w2 = pltpu.make_async_copy(wout_hbm.at[0], w2.at[mine_w2], load_sem.at[2])
    cp_th = pltpu.make_async_copy(th_hbm, heads.at[z, c, 0], load_sem.at[3])
    cp_sh = pltpu.make_async_copy(sh_hbm, heads.at[z, c, 1], load_sem.at[4])
    rw1 = remote(win_hbm.at[0], w1.at[c], w_send.at[0], w_recv.at[0], at(z, y, x, mate))
    rw2 = remote(wout_hbm.at[0], w2.at[mine_w2], w_send.at[1], w_recv.at[1], at(z, y, x, mate))
    cp_w1.start()

    def spread(row):
        return jnp.broadcast_to(row.astype(F32), (256, 256))

    pj = spread(pr_ref[...])
    pi = pj.T

    def places(expert_ref, lane):
        ej = spread(expert_ref[...])
        ei = ej.T
        same = ei == ej
        rank_row = jnp.sum(jnp.where(same & (pi < pj), 1.0, 0.0), axis=0, keepdims=True)
        rank_col = jnp.sum(jnp.where(same & (pj < pi), 1.0, 0.0), axis=1, keepdims=True)

        def place(expert, rank):
            return jnp.where(rank < CAP, (2.0 * expert + lane) * CAP + rank, -1.0)

        return place(ej[:1], rank_row), place(ei[:, :1], rank_col)

    t_row, t_col = places(te_ref, 0.0)
    s_row, s_col = places(se_ref, 1.0)
    slot = lax.broadcasted_iota(jnp.int32, (768, 256), 0).astype(F32)
    gather = jnp.where((slot == t_row) | (slot == s_row), 1.0, 0.0).astype(BF)
    lanes = lax.broadcasted_iota(jnp.int32, (256, 768), 1).astype(F32)
    pick[0:256] = jnp.where(lanes == t_col, 1.0, 0.0).astype(BF)
    pick[256:512] = jnp.where(lanes == s_col, 1.0, 0.0).astype(BF)
    cp_tok.wait()
    picked = jnp.dot(gather, tok[...], preferred_element_type=F32)
    out_rows[...] = picked.reshape(96, 8, 256).astype(BF)
    pl.semaphore_wait(barrier, jnp.where(home == c, 95, 97))

    my_slot = pl.ds(3 * lax.rem(e, 16), 3)

    def disp(to):
        return remote(
            out_rows.at[pl.ds(3 * to, 3)], feats.at[x, c, my_slot],
            disp_send.at[to], disp_recv.at[lax.rem(e, 16), c], (to, x * 2 + home),
        )

    cp_self = pltpu.make_async_copy(
        out_rows.at[pl.ds(3 * e, 3)], feats.at[x, c, my_slot], load_sem.at[5]
    )

    @pl.when(home == c)
    def _():
        cp_self.start()

    @pl.when(home != c)
    def _():
        disp(e).start()

    def send_rows(r, carry):
        disp(lax.rem(e + r, 32)).start()
        return carry

    lax.fori_loop(1, 32, send_rows, 0)
    rw1.start()
    rw2.start()
    cp_w2.start()
    cp_th.start()
    cp_sh.start()

    def arrived_rows(cc, j):
        here = feats.at[x, cc, pl.ds(3 * j, 3)]
        return remote(
            here, here, disp_send.at[0], disp_recv.at[j, cc], at(z, y, x, mate)
        )

    def wait_rows(cc):
        def wait_one(j, carry):
            @pl.when(jnp.logical_not((c * 16 + j == e) & (cc == c)))
            def _():
                arrived_rows(cc, j).wait_recv()

            return carry

        lax.fori_loop(0, 16, wait_one, 0)

    @pl.when(home == c)
    def _():
        cp_self.wait()

    def xcopy(xx, cc, k, to):
        piece = feats.at[xx, cc]
        return remote(piece, piece, xag_send.at[k], xag_recv.at[k], at(z, y, to, c))

    wait_rows(0)
    xcopy(x, 0, 0, xr).start()
    wait_rows(1)
    xcopy(x, 1, 1, xl).start()
    xcopy(x, 1, 2, xr).start()
    xcopy(x, 0, 3, xl).start()

    zu, zd = step(z, 1, 8), step(z, -1, 8)
    cp_th.wait()
    cp_sh.wait()

    def ring_up(zz, k, both):
        piece = heads.at[zz, c] if both else heads.at[zz, c, 0]
        return remote(piece, piece, hd_send.at[0, k], hd_recv.at[0, k], at(zu, y, x, c))

    def ring_down(zz, k, both):
        piece = heads.at[zz, c] if both else heads.at[zz, c, 1]
        return remote(piece, piece, hd_send.at[1, k], hd_recv.at[1, k], at(zd, y, x, c))

    def to_mate(zz, cc, k):
        piece = heads.at[zz, cc]
        return remote(piece, piece, hp_send.at[k], hp_recv.at[k], at(z, y, x, mate))

    ring_up(z, 0, True).start()
    ring_down(z, 0, True).start()
    to_mate(z, c, 0).start()

    cp_w1.wait()
    rw1.wait_recv()

    def flatten(xx):
        xin[xx] = jnp.concatenate(
            [feats[xx, cc].astype(F32).reshape(384, 256).astype(BF) for cc in (0, 1)], axis=1
        )

    def hidden_pass(xs, first, last):
        for xx in xs:
            flatten(xx)

        def body(n, carry):
            cc, m = n // 2, lax.rem(n, 2)
            cols = pl.ds(pl.multiple_of(m * 512, 512), 512)
            total = None if first else acc[cc, :, cols]
            for xx in xs:
                k = pl.ds(pl.multiple_of(xx * 512, 512), 512)
                term = jnp.dot(xin[xx], w1[cc, k, cols], preferred_element_type=F32)
                total = term if total is None else total + term
            if last:
                hid[:, pl.ds(pl.multiple_of(n * 512, 512), 512)] = gelu(total).astype(BF)
            else:
                acc[cc, :, cols] = total
            return carry

        lax.fori_loop(0, 4, body, 0)

    hidden_pass([x], True, False)
    xcopy(xl, 0, 0, xr).wait_recv()
    xcopy(xl, 0, 4, xr).start()
    xcopy(xr, 1, 1, xl).wait_recv()
    xcopy(xr, 1, 5, xl).start()
    xcopy(xl, 1, 2, xr).wait_recv()
    xcopy(xr, 0, 3, xl).wait_recv()
    hidden_pass([xl, xr], False, False)
    xcopy(xo, 0, 4, xr).wait_recv()
    xcopy(xo, 1, 5, xl).wait_recv()

    def ring_next(k):
        lo, hi = step(z, -k, 8), step(z, k, 8)
        ring_up(lo, k - 1, True).wait_recv()
        ring_down(hi, k - 1, True).wait_recv()
        ring_up(lo, k, k < 3).start()
        ring_down(hi, k, k < 3).start()
        to_mate(lo, c, 2 * k - 1).start()
        to_mate(hi, c, 2 * k).start()

    ring_next(1)
    hidden_pass([xo], False, True)

    cp_w2.wait()
    rw2.wait_recv()

    def partial(xx):
        cols = pl.ds(pl.multiple_of(xx * 512, 512), 512)
        return jnp.dot(hid[...], w2[:, cols], preferred_element_type=F32)

    def rs(k, to):
        return remote(
            part_send.at[k], part_recv.at[k], rs_send.at[k], rs_recv.at[k], at(z, y, to, c)
        )

    far = partial(xo).astype(BF)
    part_send[0] = far[:, :256]
    part_send[1] = far[:, 256:]
    rs(0, xr).start()
    rs(1, xl).start()
    own_part[1] = partial(xr)
    part_send[2] = own_part[1, :, 256:].astype(BF)
    rs(2, xr).start()
    own_part[2] = partial(xl)
    part_send[3] = own_part[2, :, :256].astype(BF)
    rs(3, xl).start()
    own_part[0] = partial(x)
    rs(0, xr).wait_recv()
    part_send[4] = (own_part[1, :, :256] + part_recv[0].astype(F32)).astype(BF)
    rs(4, xr).start()
    rs(1, xl).wait_recv()
    part_send[5] = (own_part[2, :, 256:] + part_recv[1].astype(F32)).astype(BF)
    rs(5, xl).start()
    rs(2, xr).wait_recv()
    rs(3, xl).wait_recv()

    def comb(b, cc):
        return remote(
            back.at[cc, pl.ds(3 * lax.rem(b, 16), 3)], ret.at[pl.ds(3 * e, 3)],
            comb_send.at[cc, lax.rem(b, 16)], comb_recv.at[e], (b, x * 2 + cc),
        )

    def send_back(cc):
        def one(r, carry):
            b = c * 16 + lax.rem(e + r, 16)

            @pl.when(jnp.logical_not((b == e) & (cc == c)))
            def _():
                comb(b, cc).start()

            return carry

        lax.fori_loop(0, 16, one, 0)

    rs(4, xr).wait_recv()
    total = own_part[0, :, :256] + part_recv[3].astype(F32) + part_recv[4].astype(F32)
    back[0] = total.reshape(48, 8, 256).astype(BF)
    send_back(0)
    rs(5, xl).wait_recv()
    total = own_part[0, :, 256:] + part_recv[2].astype(F32) + part_recv[5].astype(F32)
    back[1] = total.reshape(48, 8, 256).astype(BF)
    send_back(1)
    cp_back = pltpu.make_async_copy(
        back.at[c, pl.ds(3 * lax.rem(e, 16), 3)], ret.at[pl.ds(3 * e, 3)], load_sem.at[6]
    )

    @pl.when(home == c)
    def _():
        cp_back.start()
        cp_back.wait()

    def wait_back(r, carry):
        @pl.when(jnp.logical_not((r == e) & (home == c)))
        def _():
            here = ret.at[pl.ds(3 * r, 3)]
            remote(
                here, here, comb_send.at[0, 0], comb_recv.at[r], at(z, y, x, mate)
            ).wait_recv()

        return carry

    lax.fori_loop(0, 32, wait_back, 0)
    ring_next(2)

    rows = ret[...].astype(F32).reshape(768, 256).astype(BF)
    stream = tok[...].astype(F32)
    squares = []
    cols = pl.ds(pl.multiple_of(v * 256, 256), 256)
    for k, gain_ref in enumerate((tg_ref, sg_ref)):
        branch = jnp.dot(
            pick[256 * k : 256 * k + 256], rows, preferred_element_type=F32
        )
        summed = stream + branch
        scaled = (summed * gain_ref[:, cols]).astype(BF)
        unit[0, 128 * k : 128 * k + 128] = scaled[:128]
        unit[1, 128 * k : 128 * k + 128] = scaled[128:]
        column = jnp.sum(summed * summed, axis=1, keepdims=True)
        squares.append(jnp.broadcast_to(column, (256, 128)).T[:1])
    low = lax.broadcasted_iota(jnp.int32, (16, 256), 0) == 0
    for h in (0, 1):
        lines = []
        for k in (0, 1):
            part = squares[k][:, 128 * h : 128 * h + 128]
            top = part.astype(BF).astype(F32)
            lines.append(
                jnp.broadcast_to(jnp.concatenate([top, part - top], axis=1), (16, 256))
            )
        unit[h, 256:272] = jnp.where(low, lines[0], lines[1]).astype(BF)
    swap = remote(
        unit.at[mate], units.at[y, x, c], pair_send.at[0], pair_recv.at[0], at(z, y, x, mate)
    )
    swap.start()
    cp_unit = pltpu.make_async_copy(unit.at[c], units.at[y, x, c], load_sem.at[7])
    cp_unit.start()
    cp_unit.wait()
    remote(
        unit.at[mate], units.at[y, x, mate], pair_send.at[0], pair_recv.at[0],
        at(z, y, x, mate),
    ).wait_recv()

    here = (x, y)

    def place_of(axis, a, b):
        return units.at[b, a, 0] if axis == 0 else units.at[a, b, 1]

    def dev_of(axis, d):
        p, q = (step(x, d, 4), y) if axis == 0 else (x, step(y, d, 4))
        return at(z, q, p, c)

    def hop(axis, along, a, b, k, d, rows_=None):
        piece = place_of(axis, a, b)
        if rows_ is not None:
            piece = piece.at[rows_[0] : rows_[1]]
        return remote(piece, piece, ag_send.at[axis, k], ag_recv.at[axis, k], dev_of(along, d))

    halves = ((0, 128), (128, 272))

    def first(axis, k, off, d, rows_=None):
        a = step(here[axis], off, 4)
        return hop(axis, axis, a, here[1 - axis], k, d, rows_)

    def second(axis, rel, off, kind, d):
        a = step(here[axis], rel, 4)
        b = step(here[1 - axis], off, 4)
        return hop(axis, 1 - axis, a, b, 4 + 3 * rel + kind, d)

    both = (0, 1)
    for axis in both:
        first(axis, 0, 0, 1).start()
        first(axis, 1, 0, -1).start()
    for axis in both:
        second(axis, 0, 0, 0, 1).start()
        second(axis, 0, 0, 1, -1).start()
    for axis in both:
        first(axis, 0, -1, 1).wait_recv()
        first(axis, 2, -1, 1, halves[0]).start()
        first(axis, 1, 1, -1).wait_recv()
        first(axis, 3, 1, -1, halves[1]).start()
    for axis in both:
        for rel in (3, 1):
            second(axis, rel, 0, 0, 1).start()
            second(axis, rel, 0, 1, -1).start()
    for axis in both:
        first(axis, 2, 2, 1, halves[0]).wait_recv()
        first(axis, 3, 2, -1, halves[1]).wait_recv()
        second(axis, 2, 0, 0, 1).start()
        second(axis, 2, 0, 1, -1).start()
    for rel in (0, 3, 1, 2):
        for axis in both:
            second(axis, rel, -1, 0, 1).wait_recv()
            second(axis, rel, 1, 1, -1).wait_recv()
            if rel in (0, 1):
                second(axis, rel, -1, 2, 1).start()
            else:
                second(axis, rel, 1, 2, -1).start()
        if rel == 3:
            ring_next(3)
    ring_up(step(z, 4, 8), 3, False).wait_recv()
    ring_down(step(z, 4, 8), 3, False).wait_recv()
    to_mate(step(z, 4, 8), c, 7).start()
    for k in range(8):
        off = 0 if k == 0 else (4 if k == 7 else ((k + 1) // 2) * (-1 if k % 2 else 1))
        to_mate(step(z, off, 8), mate, k).wait_recv()
    for rel in (0, 3, 1, 2):
        for axis in both:
            second(axis, rel, 2, 2, 1 if rel in (0, 1) else -1).wait_recv()

    for pair in (0, 1):
        scales = []
        for k in (0, 1):
            parts = []
            for yy in (2 * pair, 2 * pair + 1):
                total = jnp.zeros((1, 128), F32)
                for xx in range(4):
                    for cc in (0, 1):
                        line = units[yy, xx, cc, 256:272, :].astype(F32)[k : k + 1]
                        total = total + line[:, :128] + line[:, 128:]
                parts.append(lax.rsqrt(total * (1.0 / 2048.0) + 1e-5))
            scales.append(jnp.concatenate(parts, axis=1))

        def logits(k, zz):
            left = heads[pl.ds(zz, 4), :, k].reshape(512, 2048)
            total = None
            for xx in range(4):
                for cc in (0, 1):
                    right = jnp.concatenate(
                        [
                            units[2 * pair + i, xx, cc, 128 * k : 128 * k + 128, :]
                            for i in (0, 1)
                        ],
                        axis=0,
                    )
                    kk = (xx * 2 + cc) * 256
                    term = lax.dot_general(
                        left[:, kk : kk + 256], right, NT, preferred_element_type=F32
                    )
                    total = term if total is None else total + term
            return total * scales[k]

        def chunk(n, carry):
            tm, ts, tw, sm, ss = carry
            tl = logits(0, 4 * n)
            sl = logits(1, 4 * n)
            tm2 = jnp.maximum(tm, jnp.max(tl, axis=0, keepdims=True))
            sm2 = jnp.maximum(sm, jnp.max(sl, axis=0, keepdims=True))
            te = jnp.exp(tl - tm2)
            keep = jnp.exp(tm - tm2)
            ts2 = ts * keep + jnp.sum(te, axis=0, keepdims=True)
            tw2 = tw * keep + jnp.sum(te * (tl - sl), axis=0, keepdims=True)
            ss2 = ss * jnp.exp(sm - sm2) + jnp.sum(jnp.exp(sl - sm2), axis=0, keepdims=True)
            return tm2, ts2, tw2, sm2, ss2

        low_row = jnp.full((1, 256), -1e30, F32)
        zero = jnp.zeros((1, 256), F32)
        stats = lax.fori_loop(0, 2, chunk, (low_row, zero, zero, low_row, zero))
        table = jnp.concatenate(list(stats) + [zero, zero, zero], axis=0)
        st_send[2 * pair] = table[:, :128]
        st_send[2 * pair + 1] = table[:, 128:]

    me = 4 * y + x

    def st_copy(r):
        yy = lax.rem(y + r // 8, 4)
        vv = lax.rem(v + lax.rem(r, 8), 8)
        return remote(
            st_send.at[yy], st_recv.at[c, me], st_ssem.at[r], st_rsem.at[c, me],
            (z * 4 + yy, vv),
        )

    def send_stats(r, carry):
        st_copy(r).start()
        return carry

    lax.fori_loop(1, 32, send_stats, 0)
    cp_st = pltpu.make_async_copy(st_send.at[y], st_recv.at[c, me], load_sem.at[8])
    cp_st.start()
    cp_st.wait()

    def wait_stats(r, carry):
        cc, k = r // 16, lax.rem(r, 16)

        @pl.when(jnp.logical_not((cc == c) & (k == me)))
        def _():
            remote(
                st_send.at[0], st_recv.at[cc, k], st_ssem.at[0], st_rsem.at[cc, k],
                at(z, y, x, mate),
            ).wait_recv()

        return carry

    lax.fori_loop(0, 32, wait_stats, 0)
    for cc in (0, 1):
        pieces = st_recv[cc]
        tm, sm = pieces[:, 0], pieces[:, 3]
        tmax = jnp.max(tm, axis=0, keepdims=True)
        smax = jnp.max(sm, axis=0, keepdims=True)
        tk, sk = jnp.exp(tm - tmax), jnp.exp(sm - smax)
        ts = jnp.sum(pieces[:, 1] * tk, axis=0, keepdims=True)
        tw = jnp.sum(pieces[:, 2] * tk, axis=0, keepdims=True)
        ss = jnp.sum(pieces[:, 4] * sk, axis=0, keepdims=True)
        o_ref[cc : cc + 1, :] = tw / ts - tmax - jnp.log(ts) + smax + jnp.log(ss)

    rw1.wait_send()
    rw2.wait_send()

    @pl.when(home != c)
    def _():
        disp(e).wait_send()

    def sent_rows(r, carry):
        disp(lax.rem(e + r, 32)).wait_send()
        return carry

    lax.fori_loop(1, 32, sent_rows, 0)
    for k in range(6):
        xcopy(x, 0, k, xr).wait_send()
        rs(k, xr).wait_send()

    def sent_back(r, carry):
        for cc in (0, 1):
            b = c * 16 + lax.rem(e + r, 16)

            @pl.when(jnp.logical_not((b == e) & (cc == c)))
            def _():
                comb(b, cc).wait_send()

        return carry

    lax.fori_loop(0, 16, sent_back, 0)
    swap.wait_send()
    for axis in both:
        first(axis, 0, 0, 1).wait_send()
        first(axis, 1, 0, -1).wait_send()
        first(axis, 2, -1, 1, halves[0]).wait_send()
        first(axis, 3, 1, -1, halves[1]).wait_send()
        for k in range(4, 16):
            hop(axis, axis, x, y, k, 1).wait_send()
    for k in range(4):
        ring_up(z, k, k < 3).wait_send()
        ring_down(z, k, k < 3).wait_send()
    for k in range(8):
        to_mate(z, c, k).wait_send()

    def sent_stats(r, carry):
        st_copy(r).wait_send()
        return carry

    lax.fori_loop(1, 32, sent_stats, 0)


def local(
    tokens, teacher_expert, student_expert, priority, expert_in, expert_out,
    teacher_gain, student_gain, teacher_head, student_head,
):
    dma = pltpu.SemaphoreType.DMA
    vm = pltpu.VMEM
    whole = pl.BlockSpec(memory_space=pltpu.VMEM)
    out = pl.pallas_call(
        kernel,
        out_shape=jax.ShapeDtypeStruct((2, 128), F32),
        in_specs=[
            pl.BlockSpec(memory_space=pl.ANY), whole, whole, whole,
            pl.BlockSpec(memory_space=pl.ANY), pl.BlockSpec(memory_space=pl.ANY),
            whole, whole,
            pl.BlockSpec(memory_space=pl.ANY), pl.BlockSpec(memory_space=pl.ANY),
        ],
        out_specs=whole,
        scratch_shapes=[
            vm((256, 256), BF),
            vm((96, 8, 256), BF),
            vm((4, 2, 48, 8, 256), BF),
            vm((2, 2048, 1024), BF),
            vm((2048, 2048), BF),
            vm((2, 384, 1024), F32),
            vm((384, 2048), BF),
            vm((6, 384, 256), BF),
            vm((6, 384, 256), BF),
            vm((3, 384, 512), F32),
            vm((4, 384, 512), BF),
            vm((2, 48, 8, 256), BF),
            vm((96, 8, 256), BF),
            vm((2, 272, 256), BF),
            vm((4, 4, 2, 272, 256), BF),
            vm((8, 2, 2, 64, 2048), BF),
            vm((4, 8, 128), F32),
            vm((2, 16, 8, 128), F32),
            vm((512, 768), BF),
            dma((9,)),
            dma((2,)), dma((2,)),
            dma((32,)), dma((16, 2)),
            dma((6,)), dma((6,)),
            dma((6,)), dma((6,)),
            dma((2, 16)), dma((32,)),
            dma((1,)), dma((1,)),
            dma((2, 16)), dma((2, 16)),
            dma((2, 4)), dma((2, 4)),
            dma((8,)), dma((8,)),
            dma((32,)), dma((2, 16)),
        ],
        compiler_params=pltpu.CompilerParams(
            has_side_effects=True, collective_id=0, vmem_limit_bytes=64 * 1024 * 1024 - 65536
        ),
    )(
        tokens,
        teacher_expert.reshape(1, -1),
        student_expert.reshape(1, -1),
        priority,
        expert_in,
        expert_out,
        teacher_gain.reshape(1, -1),
        student_gain.reshape(1, -1),
        teacher_head,
        student_head,
    )
    return out.reshape(256)


def solution(mesh):
    placed = (
        P("expert", None),
        P("expert", None),
        P("expert", None),
        P("expert", None),
        P("expert", None, "vocab"),
        P("expert", "vocab", None),
        P(),
        P(),
        P(("vocab", "expert"), None),
        P(("vocab", "expert"), None),
    )
    return jax.shard_map(local, mesh=mesh, in_specs=placed, out_specs=P("expert"), check_vma=False)
```

```python
import jax
import jax.numpy as jnp
from jax import lax
from jax.experimental import pallas as pl
from jax.experimental.pallas import tpu as pltpu
from jax.sharding import PartitionSpec as P

MESH = pl.DeviceIdType.MESH
BF = jnp.bfloat16
F32 = jnp.float32
CAP = 24
NT = (((1,), (1,)), ((), ()))


def gelu(v):
    return 0.5 * v * (1.0 + jnp.tanh(0.7978845608028654 * (v + 0.044715 * v * v * v)))


def kernel(
    tok_hbm, te_hbm, se_hbm, pr_hbm, win_hbm, wout_hbm, tg_hbm, sg_hbm, th_hbm, sh_hbm,
    o_ref,
    ids, gains,
    tok, out_rows, feats, w1, w2, acc, hid, part_send, part_recv, own_part, xin,
    back, ret, unit, units, heads, st_send, st_recv, pick, factor,
    load_sem, w_send, w_recv, disp_send, disp_recv, xag_send, xag_recv,
    rs_send, rs_recv, comb_send, comb_recv, pair_send, pair_recv,
    ag_send, ag_recv, hd_send, hd_recv, hp_send, hp_recv, st_ssem, st_rsem,
):
    e = lax.axis_index("expert")
    v = lax.axis_index("vocab")
    z, y = e // 4, e % 4
    x, c = v // 2, v % 2
    mate = 1 - c
    home = e // 16

    def at(zz, yy, xx, cc):
        return (zz * 4 + yy, xx * 2 + cc)

    def step(a, d, n):
        return lax.rem(a + d + n, n)

    xr, xl, xo = step(x, 1, 4), step(x, -1, 4), step(x, 2, 4)

    def remote(src, dst, ssem, rsem, dev):
        return pltpu.make_async_remote_copy(
            src_ref=src, dst_ref=dst, send_sem=ssem, recv_sem=rsem,
            device_id=dev, device_id_type=MESH,
        )

    cp_tok = pltpu.make_async_copy(
        tok_hbm.at[:, pl.ds(pl.multiple_of(v * 256, 256), 256)], tok, load_sem.at[0]
    )
    cp_ids = [
        pltpu.make_async_copy(src, ids.at[k], load_sem.at[5 + k])
        for k, src in enumerate((te_hbm, se_hbm, pr_hbm))
    ]
    cols = pl.ds(pl.multiple_of(v * 256, 256), 256)
    cp_gains = [
        pltpu.make_async_copy(src.at[:, cols], gains.at[k], load_sem.at[8 + k])
        for k, src in enumerate((tg_hbm, sg_hbm))
    ]
    for cp in cp_ids:
        cp.start()
    cp_tok.start()
    for cp in cp_gains:
        cp.start()
    mine_w2 = pl.ds(pl.multiple_of(c * 1024, 1024), 1024)
    cp_w1 = pltpu.make_async_copy(win_hbm.at[0], w1.at[c], load_sem.at[1])
    cp_w2 = pltpu.make_async_copy(wout_hbm.at[0], w2.at[mine_w2], load_sem.at[2])
    cp_th = pltpu.make_async_copy(th_hbm, heads.at[z, c, 0], load_sem.at[3])
    cp_sh = pltpu.make_async_copy(sh_hbm, heads.at[z, c, 1], load_sem.at[4])
    rw1 = remote(win_hbm.at[0], w1.at[c], w_send.at[0], w_recv.at[0], at(z, y, x, mate))
    rw2 = remote(wout_hbm.at[0], w2.at[mine_w2], w_send.at[1], w_recv.at[1], at(z, y, x, mate))

    barrier = pltpu.get_barrier_semaphore()

    def greet(ee, vv):
        @pl.when(jnp.logical_not((ee == e) & (vv == v)))
        def _():
            pl.semaphore_signal(barrier, inc=1, device_id=(ee, vv), device_id_type=MESH)

    def greet_rows(r, carry):
        far = lax.rem(e + 16 + r, 32)
        greet(far, x * 2 + home)
        greet(c * 16 + lax.rem(e + r, 16), x * 2 + r // 16)
        greet(z * 4 + r // 8, lax.rem(r, 8))
        return carry

    lax.fori_loop(0, 32, greet_rows, 0)
    greet(step(z, 1, 8) * 4 + y, v)
    greet(step(z, -1, 8) * 4 + y, v)

    cp_w1.start()
    for cp in cp_ids:
        cp.wait()

    def spread(row):
        return jnp.broadcast_to(row.astype(F32), (256, 256))

    pj = spread(ids[2])
    pi = pj.T

    def places(expert, lane):
        ej = spread(expert)
        ei = ej.T
        same = ei == ej
        rank_row = jnp.sum(jnp.where(same & (pi < pj), 1.0, 0.0), axis=0, keepdims=True)
        rank_col = jnp.sum(jnp.where(same & (pj < pi), 1.0, 0.0), axis=1, keepdims=True)

        def place(expert, rank):
            return jnp.where(rank < CAP, (2.0 * expert + lane) * CAP + rank, -1.0)

        return place(ej[:1], rank_row), place(ei[:, :1], rank_col)

    t_row, t_col = places(ids[0], 0.0)
    s_row, s_col = places(ids[1], 1.0)
    slot = lax.broadcasted_iota(jnp.int32, (768, 256), 0).astype(F32)
    gather = jnp.where((slot == t_row) | (slot == s_row), 1.0, 0.0).astype(BF)
    lanes = lax.broadcasted_iota(jnp.int32, (256, 768), 1).astype(F32)
    pick[0:256] = jnp.where(lanes == t_col, 1.0, 0.0).astype(BF)
    pick[256:512] = jnp.where(lanes == s_col, 1.0, 0.0).astype(BF)
    cp_tok.wait()
    for cp in cp_gains:
        cp.wait()
    picked = jnp.dot(gather, tok[...], preferred_element_type=F32)
    out_rows[0] = picked[:, :128].reshape(96, 8, 128).astype(BF)
    out_rows[1] = picked[:, 128:].reshape(96, 8, 128).astype(BF)
    pl.semaphore_wait(barrier, jnp.where(home == c, 95, 97))

    my_slot = pl.ds(3 * lax.rem(e, 16), 3)

    def disp(to, h):
        return remote(
            out_rows.at[h, pl.ds(3 * to, 3)], feats.at[x, c, h, my_slot],
            disp_send.at[h], disp_recv.at[h], (to, x * 2 + home),
        )

    cp_self = [
        pltpu.make_async_copy(
            out_rows.at[h, pl.ds(3 * e, 3)], feats.at[x, c, h, my_slot], disp_recv.at[h]
        )
        for h in (0, 1)
    ]

    for h in (0, 1):

        @pl.when(home == c)
        def _():
            cp_self[h].start()

        @pl.when(home != c)
        def _():
            disp(e, h).start()

        def send_rows(r, carry):
            disp(lax.rem(e + r, 32), h).start()
            return carry

        lax.fori_loop(1, 32, send_rows, 0)
    rw1.start()
    rw2.start()
    cp_w2.start()
    cp_th.start()
    cp_sh.start()

    def wait_rows(h):
        here = feats.at[x, :, h]
        remote(
            here, here, disp_send.at[h], disp_recv.at[h], at(z, y, x, mate)
        ).wait_recv()

    def xcopy(xx, cc, h, k, to):
        piece = feats.at[xx, cc, h]
        return remote(piece, piece, xag_send.at[0], xag_recv.at[h, k], at(z, y, to, c))

    for h in (0, 1):
        wait_rows(h)
        xcopy(x, 0, h, 0, xr).start()
        xcopy(x, 1, h, 1, xl).start()
        xcopy(x, 1, h, 2, xr).start()
        xcopy(x, 0, h, 3, xl).start()

    zu, zd = step(z, 1, 8), step(z, -1, 8)
    cp_th.wait()
    cp_sh.wait()

    def ring_up(zz, k, both):
        piece = heads.at[zz, c] if both else heads.at[zz, c, 0]
        return remote(piece, piece, hd_send.at[0], hd_recv.at[0, k], at(zu, y, x, c))

    def ring_down(zz, k, both):
        piece = heads.at[zz, c] if both else heads.at[zz, c, 1]
        return remote(piece, piece, hd_send.at[0], hd_recv.at[1, k], at(zd, y, x, c))

    def to_mate(zz, cc, k):
        piece = heads.at[zz, cc]
        return remote(piece, piece, hp_send.at[0], hp_recv.at[k], at(z, y, x, mate))

    ring_up(z, 0, True).start()
    ring_down(z, 0, True).start()
    to_mate(z, c, 0).start()

    cp_w1.wait()
    rw1.wait_recv()

    def flatten(xx):
        xin[xx] = jnp.concatenate(
            [
                feats[xx, cc, h].astype(F32).reshape(384, 128).astype(BF)
                for cc in (0, 1)
                for h in (0, 1)
            ],
            axis=1,
        )

    def hidden_pass(xs, first, last):
        for xx in xs:
            flatten(xx)

        def body(n, carry):
            cc, m = n // 2, lax.rem(n, 2)
            cols = pl.ds(pl.multiple_of(m * 512, 512), 512)
            total = None if first else acc[cc, :, cols]
            for xx in xs:
                k = pl.ds(pl.multiple_of(xx * 512, 512), 512)
                term = jnp.dot(xin[xx], w1[cc, k, cols], preferred_element_type=F32)
                total = term if total is None else total + term
            if last:
                hid[:, pl.ds(pl.multiple_of(n * 512, 512), 512)] = gelu(total).astype(BF)
            else:
                acc[cc, :, cols] = total
            return carry

        lax.fori_loop(0, 4, body, 0)

    hidden_pass([x], True, False)
    for h in (0, 1):
        xcopy(xl, 0, h, 0, xr).wait_recv()
        xcopy(xl, 0, h, 4, xr).start()
        xcopy(xr, 1, h, 1, xl).wait_recv()
        xcopy(xr, 1, h, 5, xl).start()
        xcopy(xl, 1, h, 2, xr).wait_recv()
        xcopy(xr, 0, h, 3, xl).wait_recv()
    hidden_pass([xl, xr], False, False)
    for h in (0, 1):
        xcopy(xo, 0, h, 4, xr).wait_recv()
        xcopy(xo, 1, h, 5, xl).wait_recv()

    def ring_next(k):
        lo, hi = step(z, -k, 8), step(z, k, 8)
        ring_up(lo, k - 1, True).wait_recv()
        ring_down(hi, k - 1, True).wait_recv()
        ring_up(lo, k, k < 3).start()
        ring_down(hi, k, k < 3).start()
        to_mate(lo, c, 1).start()
        to_mate(hi, c, 0).start()

    ring_next(1)
    hidden_pass([xo], False, True)

    cp_w2.wait()
    rw2.wait_recv()

    def partial(xx):
        cols = pl.ds(pl.multiple_of(xx * 512, 512), 512)
        return jnp.dot(hid[...], w2[:, cols], preferred_element_type=F32)

    def rs(h, k, to):
        return remote(
            part_send.at[h, k], part_recv.at[h, k], rs_send.at[0], rs_recv.at[h, k],
            at(z, y, to, c),
        )

    far = partial(xo).astype(BF)
    for h in (0, 1):
        part_send[h, 0] = far[:192, 256 * h : 256 * h + 256]
        part_send[h, 1] = far[192:, 256 * h : 256 * h + 256]
    rs(0, 0, xr).start()
    rs(0, 1, xl).start()
    own_part[1] = partial(xr)
    for h in (0, 1):
        part_send[h, 2] = own_part[1, 192:, 256 * h : 256 * h + 256].astype(BF)
    rs(0, 2, xr).start()
    own_part[2] = partial(xl)
    for h in (0, 1):
        part_send[h, 3] = own_part[2, :192, 256 * h : 256 * h + 256].astype(BF)
    rs(0, 3, xl).start()

    def merge(h):
        half = slice(256 * h, 256 * h + 256)
        rs(h, 0, xr).wait_recv()
        part_send[h, 4] = (own_part[1, :192, half] + part_recv[h, 0].astype(F32)).astype(BF)
        rs(h, 4, xr).start()
        rs(h, 1, xl).wait_recv()
        part_send[h, 5] = (own_part[2, 192:, half] + part_recv[h, 1].astype(F32)).astype(BF)
        rs(h, 5, xl).start()

    merge(0)
    rs(1, 0, xr).start()
    rs(1, 1, xl).start()
    rs(1, 2, xr).start()
    rs(1, 3, xl).start()
    own_part[0] = partial(x)

    def comb(b, cc):
        return remote(
            back.at[cc, pl.ds(3 * lax.rem(b, 16), 3)], ret.at[pl.ds(3 * e, 3)],
            comb_send.at[cc], comb_recv.at[0], (b, x * 2 + cc),
        )

    def send_back(cc):
        def one(r, carry):
            b = c * 16 + lax.rem(e + r, 16)

            @pl.when(jnp.logical_not((b == e) & (cc == c)))
            def _():
                comb(b, cc).start()

            return carry

        lax.fori_loop(0, 16, one, 0)

    def collect(h):
        half = slice(256 * h, 256 * h + 256)
        for rows_, near, merged in ((slice(0, 192), 3, 4), (slice(192, 384), 2, 5)):
            rs(h, near, xr).wait_recv()
            rs(h, merged, xr).wait_recv()
            total = (
                own_part[0, rows_, half]
                + part_recv[h, near].astype(F32)
                + part_recv[h, merged].astype(F32)
            )
            back[h, rows_.start // 8 : rows_.stop // 8] = total.reshape(24, 8, 256).astype(BF)
        send_back(h)

    collect(0)
    merge(1)
    collect(1)
    cp_back = pltpu.make_async_copy(
        back.at[c, pl.ds(3 * lax.rem(e, 16), 3)], ret.at[pl.ds(3 * e, 3)], comb_recv.at[0]
    )

    @pl.when(home == c)
    def _():
        cp_back.start()

    swap = remote(
        unit, units.at[y, x, c], pair_send.at[0], pair_recv.at[0], at(z, y, x, mate)
    )
    from_mate = remote(
        unit, units.at[y, x, mate], pair_send.at[0], pair_recv.at[0], at(z, y, x, mate)
    )

    def finish(core):
        pltpu.make_async_copy(ret, ret, comb_recv.at[0]).wait()
        rows = ret[...].astype(F32).reshape(768, 256).astype(BF)
        stream = tok[...].astype(F32)
        kept = units.at[y, x, core]
        squares = []
        for k in (0, 1):
            branch = jnp.dot(
                pick[256 * k : 256 * k + 256], rows, preferred_element_type=F32
            )
            summed = stream + branch
            scaled = (summed * gains[k]).astype(BF)
            parts = (scaled[:128], scaled[128:])
            kept[128 * k : 128 * k + 128] = parts[core]
            unit[128 * k : 128 * k + 128] = parts[1 - core]
            column = jnp.sum(summed * summed, axis=1, keepdims=True)
            squares.append(jnp.broadcast_to(column, (256, 128)).T[:1])
        low = lax.broadcasted_iota(jnp.int32, (16, 256), 0) == 0
        for h, place in ((core, kept), (1 - core, unit)):
            lines = []
            for k in (0, 1):
                part = squares[k][:, 128 * h : 128 * h + 128]
                top = part.astype(BF).astype(F32)
                lines.append(
                    jnp.broadcast_to(jnp.concatenate([top, part - top], axis=1), (16, 256))
                )
            place[256:272] = jnp.where(low, lines[0], lines[1]).astype(BF)
        swap.start()

    here = (x, y)

    def place_of(axis, a, b):
        return units.at[b, a, 0] if axis == 0 else units.at[a, b, 1]

    def dev_of(axis, d):
        p, q = (step(x, d, 4), y) if axis == 0 else (x, step(y, d, 4))
        return at(z, q, p, c)

    def hop(axis, along, a, b, k, d, rows_=None):
        piece = place_of(axis, a, b)
        if rows_ is not None:
            piece = piece.at[rows_[0] : rows_[1]]
        return remote(
            piece, piece, ag_send.at[axis, min(k // 4, 1)], ag_recv.at[axis, k], dev_of(along, d)
        )

    halves = ((0, 128), (128, 272))

    def first(axis, k, off, d, rows_=None):
        a = step(here[axis], off, 4)
        return hop(axis, axis, a, here[1 - axis], k, d, rows_)

    def second(axis, rel, off, kind, d):
        a = step(here[axis], rel, 4)
        b = step(here[1 - axis], off, 4)
        return hop(axis, 1 - axis, a, b, 4 + 3 * rel + kind, d)

    both = (0, 1)

    def begin(axis):
        @pl.when(c == axis)
        def _():
            finish(axis)

        @pl.when(c != axis)
        def _():
            from_mate.wait_recv()

        first(axis, 0, 0, 1).start()
        first(axis, 1, 0, -1).start()
        second(axis, 0, 0, 0, 1).start()
        second(axis, 0, 0, 1, -1).start()

    def forward_first(axis):
        first(axis, 0, -1, 1).wait_recv()
        first(axis, 2, -1, 1, halves[0]).start()
        first(axis, 1, 1, -1).wait_recv()
        first(axis, 3, 1, -1, halves[1]).start()

    def pass_on(axis, rel):
        second(axis, rel, 0, 0, 1).start()
        second(axis, rel, 0, 1, -1).start()

    def opposite(axis):
        first(axis, 2, 2, 1, halves[0]).wait_recv()
        first(axis, 3, 2, -1, halves[1]).wait_recv()
        pass_on(axis, 2)

    def forward_second(axis, rel):
        second(axis, rel, -1, 0, 1).wait_recv()
        second(axis, rel, 1, 1, -1).wait_recv()
        if rel in (0, 1):
            second(axis, rel, -1, 2, 1).start()
        else:
            second(axis, rel, 1, 2, -1).start()

    begin(0)
    forward_first(0)
    pass_on(0, 3)
    begin(1)
    ring_next(2)
    pass_on(0, 1)
    forward_first(1)
    pass_on(1, 3)
    pass_on(1, 1)
    opposite(0)
    opposite(1)
    for rel in (0, 3, 1, 2):
        for axis in both:
            forward_second(axis, rel)
        if rel == 3:
            ring_next(3)
    for rel in (0, 3, 1, 2):
        for axis in both:
            second(axis, rel, 2, 2, 1 if rel in (0, 1) else -1).wait_recv()
    ring_up(step(z, 4, 8), 3, False).wait_recv()
    ring_down(step(z, 4, 8), 3, False).wait_recv()
    to_mate(step(z, 4, 8), c, 1).start()

    def from_mate_heads(k):
        pltpu.make_async_copy(heads.at[0:4, 0], heads.at[0:4, 0], hp_recv.at[k]).wait()

    for yy in range(4):
        for k in (0, 1):
            total = jnp.zeros((1, 128), F32)
            for xx in range(4):
                for cc in (0, 1):
                    line = units[yy, xx, cc, 256:272, :].astype(F32)[k : k + 1]
                    total = total + line[:, :128] + line[:, 128:]
            factor[yy, k : k + 1] = lax.rsqrt(total * (1.0 / 2048.0) + 1e-5)

    def logits(pair, k, n):
        left = [heads[lax.rem(z + 4 * n + i, 8), :, k].reshape(128, 2048) for i in range(4)]
        left = jnp.concatenate(left, axis=0)
        total = None
        for xx in range(4):
            for cc in (0, 1):
                right = jnp.concatenate(
                    [
                        units[2 * pair + i, xx, cc, 128 * k : 128 * k + 128, :]
                        for i in (0, 1)
                    ],
                    axis=0,
                )
                kk = (xx * 2 + cc) * 256
                term = lax.dot_general(
                    left[:, kk : kk + 256], right, NT, preferred_element_type=F32
                )
                total = term if total is None else total + term
        scale = [factor[2 * pair + i, k : k + 1] for i in (0, 1)]
        return total * jnp.concatenate(scale, axis=1)

    def chunk(n):
        def one_pair(pair, carry):
            tl = logits(pair, 0, n)
            sl = logits(pair, 1, n)
            tm = jnp.max(tl, axis=0, keepdims=True)
            sm = jnp.max(sl, axis=0, keepdims=True)
            if n == 1:
                old = jnp.concatenate([st_send[2 * pair], st_send[2 * pair + 1]], axis=1)
                tm = jnp.maximum(tm, old[0:1])
                sm = jnp.maximum(sm, old[3:4])
            te = jnp.exp(tl - tm)
            ts = jnp.sum(te, axis=0, keepdims=True)
            tw = jnp.sum(te * (tl - sl), axis=0, keepdims=True)
            ss = jnp.sum(jnp.exp(sl - sm), axis=0, keepdims=True)
            if n == 1:
                keep = jnp.exp(old[0:1] - tm)
                ts = ts + old[1:2] * keep
                tw = tw + old[2:3] * keep
                ss = ss + old[4:5] * jnp.exp(old[3:4] - sm)
            zero = jnp.zeros((3, 256), F32)
            table = jnp.concatenate([tm, ts, tw, sm, ss, zero], axis=0)
            st_send[2 * pair] = table[:, :128]
            st_send[2 * pair + 1] = table[:, 128:]
            return carry

        lax.fori_loop(0, 2, one_pair, 0)

    from_mate_heads(0)
    chunk(0)
    from_mate_heads(1)
    chunk(1)

    me = 4 * y + x

    def st_copy(r):
        yy = lax.rem(y + r // 8, 4)
        vv = lax.rem(v + lax.rem(r, 8), 8)
        return remote(
            st_send.at[yy], st_recv.at[c, me], st_ssem.at[0], st_rsem.at[0],
            (z * 4 + yy, vv),
        )

    def send_stats(r, carry):
        st_copy(r).start()
        return carry

    lax.fori_loop(1, 32, send_stats, 0)
    pltpu.make_async_copy(st_send.at[y], st_recv.at[c, me], st_rsem.at[0]).start()

    rw1.wait_send()
    rw2.wait_send()

    for h in (0, 1):

        @pl.when(home != c)
        def _():
            pltpu.make_async_copy(out_rows.at[h], out_rows.at[h], disp_send.at[h]).wait()

        @pl.when(home == c)
        def _():
            most = out_rows.at[h, pl.ds(0, 93)]
            pltpu.make_async_copy(most, most, disp_send.at[h]).wait()

    pltpu.make_async_copy(feats.at[0:3], feats.at[0:3], xag_send.at[0]).wait()
    pltpu.make_async_copy(part_send, part_send, rs_send.at[0]).wait()

    for h in (0, 1):

        @pl.when((home == c) & (c == h))
        def _():
            most = back.at[h, pl.ds(0, 45)]
            pltpu.make_async_copy(most, most, comb_send.at[h]).wait()

        @pl.when(jnp.logical_not((home == c) & (c == h)))
        def _():
            pltpu.make_async_copy(back.at[h], back.at[h], comb_send.at[h]).wait()

    swap.wait_send()
    for axis in both:
        for k, sent in ((0, units.at[0:3, 0, 0]), (1, units.at[0:3, :, 0])):
            pltpu.make_async_copy(sent, sent, ag_send.at[axis, k]).wait()
    pltpu.make_async_copy(heads.at[0:7, 0], heads.at[0:7, 0], hd_send.at[0]).wait()
    pltpu.make_async_copy(heads.at[:, 0], heads.at[:, 0], hp_send.at[0]).wait()

    pltpu.make_async_copy(st_recv, st_recv, st_rsem.at[0]).wait()
    for cc in (0, 1):
        pieces = st_recv[cc]
        tm, sm = pieces[:, 0], pieces[:, 3]
        tmax = jnp.max(tm, axis=0, keepdims=True)
        smax = jnp.max(sm, axis=0, keepdims=True)
        tk, sk = jnp.exp(tm - tmax), jnp.exp(sm - smax)
        ts = jnp.sum(pieces[:, 1] * tk, axis=0, keepdims=True)
        tw = jnp.sum(pieces[:, 2] * tk, axis=0, keepdims=True)
        ss = jnp.sum(pieces[:, 4] * sk, axis=0, keepdims=True)
        o_ref[cc : cc + 1, :] = tw / ts - tmax - jnp.log(ts) + smax + jnp.log(ss)

    sent = out_rows.at[0, pl.ds(0, 62)]
    pltpu.make_async_copy(sent, sent, st_ssem.at[0]).wait()


def local(
    tokens, teacher_expert, student_expert, priority, expert_in, expert_out,
    teacher_gain, student_gain, teacher_head, student_head,
):
    dma = pltpu.SemaphoreType.DMA
    vm = pltpu.VMEM
    whole = pl.BlockSpec(memory_space=pltpu.VMEM)
    out = pl.pallas_call(
        kernel,
        out_shape=jax.ShapeDtypeStruct((2, 128), F32),
        in_specs=[pl.BlockSpec(memory_space=pl.ANY)] * 10,
        out_specs=whole,
        scratch_shapes=[
            vm((3, 1, 256), jnp.int32),
            vm((2, 1, 256), F32),
            vm((256, 256), BF),
            vm((2, 96, 8, 128), BF),
            vm((4, 2, 2, 48, 8, 128), BF),
            vm((2, 2048, 1024), BF),
            vm((2048, 2048), BF),
            vm((2, 384, 1024), F32),
            vm((384, 2048), BF),
            vm((2, 6, 192, 256), BF),
            vm((2, 6, 192, 256), BF),
            vm((3, 384, 512), F32),
            vm((4, 384, 512), BF),
            vm((2, 48, 8, 256), BF),
            vm((96, 8, 256), BF),
            vm((272, 256), BF),
            vm((4, 4, 2, 272, 256), BF),
            vm((8, 2, 2, 64, 2048), BF),
            vm((4, 8, 128), F32),
            vm((2, 16, 8, 128), F32),
            vm((512, 768), BF),
            vm((4, 8, 128), F32),
            dma((10,)),
            dma((2,)), dma((2,)),
            dma((2,)), dma((2,)),
            dma((1,)), dma((2, 6)),
            dma((1,)), dma((2, 6)),
            dma((2,)), dma((1,)),
            dma((1,)), dma((1,)),
            dma((2, 2)), dma((2, 16)),
            dma((1,)), dma((2, 4)),
            dma((1,)), dma((2,)),
            dma((1,)), dma((1,)),
        ],
        compiler_params=pltpu.CompilerParams(
            has_side_effects=True, collective_id=0, vmem_limit_bytes=64 * 1024 * 1024 - 65536
        ),
    )(
        tokens,
        teacher_expert.reshape(1, -1),
        student_expert.reshape(1, -1),
        priority,
        expert_in,
        expert_out,
        teacher_gain.reshape(1, -1),
        student_gain.reshape(1, -1),
        teacher_head,
        student_head,
    )
    return out.reshape(256)


def solution(mesh):
    placed = (
        P("expert", None),
        P("expert", None),
        P("expert", None),
        P("expert", None),
        P("expert", None, "vocab"),
        P("expert", "vocab", None),
        P(),
        P(),
        P(("vocab", "expert"), None),
        P(("vocab", "expert"), None),
    )
    return jax.shard_map(local, mesh=mesh, in_specs=placed, out_specs=P("expert"), check_vma=False)
```

```python
import jax
import jax.numpy as jnp
from jax import lax
from jax.experimental import pallas as pl
from jax.experimental.pallas import tpu as pltpu
from jax.sharding import PartitionSpec as P

MESH = pl.DeviceIdType.MESH
BF = jnp.bfloat16
F32 = jnp.float32
CAP = 24
NT = (((1,), (1,)), ((), ()))


def gelu(v):
    return 0.5 * v * (1.0 + jnp.tanh(0.7978845608028654 * (v + 0.044715 * v * v * v)))


def kernel(
    tok_hbm, te_hbm, se_hbm, pr_hbm, win_hbm, wout_hbm, tg_hbm, sg_hbm, th_hbm, sh_hbm,
    o_ref,
    ids, gains,
    tok, out_rows, feats, w1, w2, acc, hid, part_send, part_recv, own_part, xin,
    back, ret, unit, units, heads, st_send, st_recv, pick, factor, res,
    load_sem, w_send, w_recv, disp_send, disp_recv, xag_send, xag_recv,
    rs_send, rs_recv, comb_send, comb_recv, pair_send, pair_recv,
    ag_send, ag_recv, hd_send, hd_recv, hp_send, hp_recv, st_ssem, st_rsem,
):
    e = lax.axis_index("expert")
    v = lax.axis_index("vocab")
    z, y = e // 4, e % 4
    x, c = v // 2, v % 2
    mate = 1 - c
    home = e // 16

    def at(zz, yy, xx, cc):
        return (zz * 4 + yy, xx * 2 + cc)

    def step(a, d, n):
        return lax.rem(a + d + n, n)

    xr, xl, xo = step(x, 1, 4), step(x, -1, 4), step(x, 2, 4)

    def remote(src, dst, ssem, rsem, dev):
        return pltpu.make_async_remote_copy(
            src_ref=src, dst_ref=dst, send_sem=ssem, recv_sem=rsem,
            device_id=dev, device_id_type=MESH,
        )

    cp_tok = pltpu.make_async_copy(
        tok_hbm.at[:, pl.ds(pl.multiple_of(v * 256, 256), 256)], tok, load_sem.at[1]
    )
    cp_ids = [
        pltpu.make_async_copy(src, ids.at[k], load_sem.at[0])
        for k, src in enumerate((te_hbm, se_hbm, pr_hbm))
    ]
    cols = pl.ds(pl.multiple_of(v * 256, 256), 256)
    cp_gains = [
        pltpu.make_async_copy(src.at[:, cols], gains.at[k], load_sem.at[2])
        for k, src in enumerate((tg_hbm, sg_hbm))
    ]
    for cp in cp_ids:
        cp.start()
    cp_tok.start()
    for cp in cp_gains:
        cp.start()
    mine_w2 = pl.ds(pl.multiple_of(c * 1024, 1024), 1024)
    cp_w1 = pltpu.make_async_copy(win_hbm.at[0], w1.at[c], load_sem.at[3])
    cp_w2 = pltpu.make_async_copy(wout_hbm.at[0], w2.at[mine_w2], load_sem.at[4])
    cp_th = pltpu.make_async_copy(th_hbm, heads.at[z, c, 0], load_sem.at[5])
    cp_sh = pltpu.make_async_copy(sh_hbm, heads.at[z, c, 1], load_sem.at[5])
    rw1 = remote(win_hbm.at[0], w1.at[c], w_send.at[0], w_recv.at[0], at(z, y, x, mate))
    rw2 = remote(wout_hbm.at[0], w2.at[mine_w2], w_send.at[1], w_recv.at[1], at(z, y, x, mate))

    barrier = pltpu.get_barrier_semaphore()

    def greet(ee, vv):
        @pl.when(jnp.logical_not((ee == e) & (vv == v)))
        def _():
            pl.semaphore_signal(barrier, inc=1, device_id=(ee, vv), device_id_type=MESH)

    def greet_rows(r, carry):
        far = lax.rem(e + 16 + r, 32)
        greet(far, x * 2 + home)
        greet(c * 16 + lax.rem(e + r, 16), x * 2 + r // 16)
        greet(z * 4 + r // 8, lax.rem(r, 8))
        return carry

    lax.fori_loop(0, 32, greet_rows, 0)
    greet(step(z, 1, 8) * 4 + y, v)
    greet(step(z, -1, 8) * 4 + y, v)

    cp_w1.start()
    pltpu.make_async_copy(ids, ids, load_sem.at[0]).wait()

    def spread(row):
        return jnp.broadcast_to(row.astype(F32), (256, 256))

    pj = spread(ids[2])
    pi = pj.T

    def places(expert, lane):
        ej = spread(expert)
        ei = ej.T
        same = ei == ej
        rank_row = jnp.sum(jnp.where(same & (pi < pj), 1.0, 0.0), axis=0, keepdims=True)
        rank_col = jnp.sum(jnp.where(same & (pj < pi), 1.0, 0.0), axis=1, keepdims=True)

        def place(expert, rank):
            return jnp.where(rank < CAP, (2.0 * expert + lane) * CAP + rank, -1.0)

        return place(ej[:1], rank_row), place(ei[:, :1], rank_col)

    t_row, t_col = places(ids[0], 0.0)
    s_row, s_col = places(ids[1], 1.0)
    slot = lax.broadcasted_iota(jnp.int32, (768, 256), 0).astype(F32)
    gather = jnp.where((slot == t_row) | (slot == s_row), 1.0, 0.0).astype(BF)
    lanes = lax.broadcasted_iota(jnp.int32, (256, 768), 1).astype(F32)
    pick[0:256] = jnp.where(lanes == t_col, 1.0, 0.0).astype(BF)
    pick[256:512] = jnp.where(lanes == s_col, 1.0, 0.0).astype(BF)
    cp_tok.wait()
    pltpu.make_async_copy(gains, gains, load_sem.at[2]).wait()
    picked = jnp.dot(gather, tok[...], preferred_element_type=F32)
    out_rows[0] = picked[:, :128].reshape(96, 8, 128).astype(BF)
    out_rows[1] = picked[:, 128:].reshape(96, 8, 128).astype(BF)
    pl.semaphore_wait(barrier, jnp.where(home == c, 95, 97))

    my_slot = pl.ds(3 * lax.rem(e, 16), 3)

    far_first = [lax.rem(z + d, 8) for d in (4, 3, 5, 2, 6, 1, 7, 0)]

    def disp(to, h):
        return remote(
            out_rows.at[h, pl.ds(3 * to, 3)], feats.at[x, c, h, my_slot],
            disp_send.at[h], disp_recv.at[h], (to, x * 2 + home),
        )

    cp_self = [
        pltpu.make_async_copy(
            out_rows.at[h, pl.ds(3 * e, 3)], feats.at[x, c, h, my_slot], disp_recv.at[h]
        )
        for h in (0, 1)
    ]

    for h in (0, 1):

        @pl.when(home == c)
        def _():
            cp_self[h].start()

        @pl.when(home != c)
        def _():
            disp(e, h).start()

        for k, zz in enumerate(far_first):

            def send_rows(r, carry):
                disp(zz * 4 + lax.rem(y + 1 + r, 4), h).start()
                return carry

            lax.fori_loop(0, 3 if k == 7 else 4, send_rows, 0)
    rw1.start()
    rw2.start()
    cp_w2.start()
    cp_th.start()
    cp_sh.start()

    def wait_rows(h):
        here = feats.at[x, :, h]
        remote(
            here, here, disp_send.at[h], disp_recv.at[h], at(z, y, x, mate)
        ).wait_recv()

    def xcopy(xx, cc, h, k, to):
        piece = feats.at[xx, cc, h]
        return remote(piece, piece, xag_send.at[0], xag_recv.at[h, k], at(z, y, to, c))

    for h in (0, 1):
        wait_rows(h)
        xcopy(x, 0, h, 0, xr).start()
        xcopy(x, 1, h, 1, xl).start()
        xcopy(x, 1, h, 2, xr).start()
        xcopy(x, 0, h, 3, xl).start()

    zu, zd = step(z, 1, 8), step(z, -1, 8)
    pltpu.make_async_copy(heads.at[z, c], heads.at[z, c], load_sem.at[5]).wait()

    def ring_up(zz, k, both):
        piece = heads.at[zz, c] if both else heads.at[zz, c, 0]
        return remote(piece, piece, hd_send.at[0], hd_recv.at[0, k], at(zu, y, x, c))

    def ring_down(zz, k, both):
        piece = heads.at[zz, c] if both else heads.at[zz, c, 1]
        return remote(piece, piece, hd_send.at[0], hd_recv.at[1, k], at(zd, y, x, c))

    def to_mate(zz, cc, k):
        piece = heads.at[zz, cc]
        return remote(piece, piece, hp_send.at[0], hp_recv.at[k], at(z, y, x, mate))

    ring_up(z, 0, True).start()
    ring_down(z, 0, True).start()
    to_mate(z, c, 0).start()

    cp_w1.wait()
    rw1.wait_recv()

    def flatten(xx):
        xin[xx] = jnp.concatenate(
            [
                feats[xx, cc, h].astype(F32).reshape(384, 128).astype(BF)
                for cc in (0, 1)
                for h in (0, 1)
            ],
            axis=1,
        )

    def hidden_pass(xs, first, last):
        for xx in xs:
            flatten(xx)

        def body(n, carry):
            cc, m = n // 2, lax.rem(n, 2)
            cols = pl.ds(pl.multiple_of(m * 512, 512), 512)
            total = None if first else acc[cc, :, cols]
            for xx in xs:
                k = pl.ds(pl.multiple_of(xx * 512, 512), 512)
                term = jnp.dot(xin[xx], w1[cc, k, cols], preferred_element_type=F32)
                total = term if total is None else total + term
            if last:
                hid[:, pl.ds(pl.multiple_of(n * 512, 512), 512)] = gelu(total).astype(BF)
            else:
                acc[cc, :, cols] = total
            return carry

        lax.fori_loop(0, 4, body, 0)

    hidden_pass([x], True, False)
    for h in (0, 1):
        xcopy(xl, 0, h, 0, xr).wait_recv()
        xcopy(xl, 0, h, 4, xr).start()
        xcopy(xr, 1, h, 1, xl).wait_recv()
        xcopy(xr, 1, h, 5, xl).start()
        xcopy(xl, 1, h, 2, xr).wait_recv()
        xcopy(xr, 0, h, 3, xl).wait_recv()
    hidden_pass([xl, xr], False, False)
    for h in (0, 1):
        xcopy(xo, 0, h, 4, xr).wait_recv()
        xcopy(xo, 1, h, 5, xl).wait_recv()

    def ring_next(k):
        lo, hi = step(z, -k, 8), step(z, k, 8)
        ring_up(lo, k - 1, True).wait_recv()
        ring_down(hi, k - 1, True).wait_recv()
        ring_up(lo, k, k < 3).start()
        ring_down(hi, k, k < 3).start()
        to_mate(lo, c, 1).start()
        to_mate(hi, c, 0).start()

    hidden_pass([xo], False, True)
    ring_next(1)

    cp_w2.wait()
    rw2.wait_recv()

    def partial(xx):
        cols = pl.ds(pl.multiple_of(xx * 512, 512), 512)
        return jnp.dot(hid[...], w2[:, cols], preferred_element_type=F32)

    def rs(h, k, to):
        return remote(
            part_send.at[h, k], part_recv.at[h, k], rs_send.at[0], rs_recv.at[h, k],
            at(z, y, to, c),
        )

    far = partial(xo).astype(BF)
    for h in (0, 1):
        part_send[h, 0] = far[:192, 256 * h : 256 * h + 256]
        part_send[h, 1] = far[192:, 256 * h : 256 * h + 256]
    rs(0, 0, xr).start()
    rs(0, 1, xl).start()
    own_part[1] = partial(xr)
    for h in (0, 1):
        part_send[h, 2] = own_part[1, 192:, 256 * h : 256 * h + 256].astype(BF)
    rs(0, 2, xr).start()
    own_part[2] = partial(xl)
    for h in (0, 1):
        part_send[h, 3] = own_part[2, :192, 256 * h : 256 * h + 256].astype(BF)
    rs(0, 3, xl).start()

    def merge(h):
        half = slice(256 * h, 256 * h + 256)
        rs(h, 0, xr).wait_recv()
        part_send[h, 4] = (own_part[1, :192, half] + part_recv[h, 0].astype(F32)).astype(BF)
        rs(h, 4, xr).start()
        rs(h, 1, xl).wait_recv()
        part_send[h, 5] = (own_part[2, 192:, half] + part_recv[h, 1].astype(F32)).astype(BF)
        rs(h, 5, xl).start()

    merge(0)
    rs(1, 0, xr).start()
    rs(1, 1, xl).start()
    rs(1, 2, xr).start()
    rs(1, 3, xl).start()
    own_part[0] = partial(x)

    def comb(b, cc):
        return remote(
            back.at[cc, pl.ds(3 * lax.rem(b, 16), 3)], ret.at[pl.ds(3 * e, 3)],
            comb_send.at[cc], comb_recv.at[0], (b, x * 2 + cc),
        )

    def send_back(cc):
        for zz in far_first:

            @pl.when(zz // 4 == c)
            def _():
                def one(r, carry):
                    b = zz * 4 + lax.rem(y + 1 + r, 4)

                    @pl.when(jnp.logical_not((b == e) & (cc == c)))
                    def _():
                        comb(b, cc).start()

                    return carry

                lax.fori_loop(0, 4, one, 0)

    def collect(h):
        half = slice(256 * h, 256 * h + 256)
        for rows_, near, merged in ((slice(0, 192), 3, 4), (slice(192, 384), 2, 5)):
            rs(h, near, xr).wait_recv()
            rs(h, merged, xr).wait_recv()
            total = (
                own_part[0, rows_, half]
                + part_recv[h, near].astype(F32)
                + part_recv[h, merged].astype(F32)
            )
            back[h, rows_.start // 8 : rows_.stop // 8] = total.reshape(24, 8, 256).astype(BF)
        send_back(h)

    collect(0)
    merge(1)
    collect(1)
    cp_back = pltpu.make_async_copy(
        back.at[c, pl.ds(3 * lax.rem(e, 16), 3)], ret.at[pl.ds(3 * e, 3)], comb_recv.at[0]
    )

    @pl.when(home == c)
    def _():
        cp_back.start()

    swap = remote(
        unit, units.at[y, x, c], pair_send.at[0], pair_recv.at[0], at(z, y, x, mate)
    )
    from_mate = remote(
        unit, units.at[y, x, mate], pair_send.at[0], pair_recv.at[0], at(z, y, x, mate)
    )

    def finish(core):
        pltpu.make_async_copy(ret, ret, comb_recv.at[0]).wait()
        rows = ret[...].astype(F32).reshape(768, 256).astype(BF)
        stream = tok[...].astype(F32)
        kept = units.at[y, x, core]
        squares = []
        for k in (0, 1):
            branch = jnp.dot(
                pick[256 * k : 256 * k + 256], rows, preferred_element_type=F32
            )
            summed = stream + branch
            scaled = (summed * gains[k]).astype(BF)
            parts = (scaled[:128], scaled[128:])
            kept[128 * k : 128 * k + 128] = parts[core]
            unit[128 * k : 128 * k + 128] = parts[1 - core]
            column = jnp.sum(summed * summed, axis=1, keepdims=True)
            squares.append(jnp.broadcast_to(column, (256, 128)).T[:1])
        low = lax.broadcasted_iota(jnp.int32, (16, 256), 0) == 0
        for h, place in ((core, kept), (1 - core, unit)):
            lines = []
            for k in (0, 1):
                part = squares[k][:, 128 * h : 128 * h + 128]
                top = part.astype(BF).astype(F32)
                lines.append(
                    jnp.broadcast_to(jnp.concatenate([top, part - top], axis=1), (16, 256))
                )
            place[256:272] = jnp.where(low, lines[0], lines[1]).astype(BF)
        swap.start()

    here = (x, y)
    spans = ((0, 64, 128), (128, 192, 272))

    def dev_of(along, d):
        p, q = (step(x, d, 4), y) if along == 0 else (x, step(y, d, 4))
        return at(z, q, p, c)

    def hop(axis, half, along, a, b, k, d, ends):
        xx, yy = (a, b) if axis == 0 else (b, a)
        piece = units.at[yy, xx, half, ends[0] : ends[1]]
        return remote(
            piece, piece, ag_send.at[axis, half, min(k // 4, 1)], ag_recv.at[axis, half, k],
            dev_of(along, d),
        )

    def first(axis, half, k, off, d):
        lo, mid, hi = spans[axis]
        ends = ((lo, hi), (lo, hi), (lo, mid), (mid, hi))[k]
        a = step(here[axis], off, 4)
        return hop(axis, half, axis, a, here[1 - axis], k, d, ends)

    def second(axis, half, rel, off, kind, d):
        a = step(here[axis], rel, 4)
        b = step(here[1 - axis], off, 4)
        ends = (spans[axis][0], spans[axis][2])
        return hop(axis, half, 1 - axis, a, b, 4 + (rel if kind == 0 else 4), d, ends)

    both = (0, 1)

    def begin(half):
        @pl.when(c == half)
        def _():
            finish(half)

        @pl.when(c != half)
        def _():
            from_mate.wait_recv()

        for axis in both:
            first(axis, half, 0, 0, 1).start()
            first(axis, half, 1, 0, -1).start()
        pass_on(half, 0)

    def forward_first(half):
        for axis in both:
            first(axis, half, 0, -1, 1).wait_recv()
            first(axis, half, 2, -1, 1).start()
            first(axis, half, 1, 1, -1).wait_recv()
            first(axis, half, 3, 1, -1).start()

    def pass_on(half, rel):
        for axis in both:
            second(axis, half, rel, 0, 0, 1).start()
            second(axis, half, rel, 0, 0, -1).start()

    def opposite(half):
        for axis in both:
            first(axis, half, 2, 2, 1).wait_recv()
            first(axis, half, 3, 2, -1).wait_recv()
        pass_on(half, 2)

    def forward_second(half, rel):
        for axis in both:
            pair_of = units.at[0:2, 0, 0, spans[axis][0] : spans[axis][2]]
            pltpu.make_async_copy(
                pair_of, pair_of, ag_recv.at[axis, half, 4 + rel]
            ).wait()
            if rel in (0, 1):
                second(axis, half, rel, -1, 1, 1).start()
            else:
                second(axis, half, rel, 1, 1, -1).start()

    begin(0)
    forward_first(0)
    pass_on(0, 3)
    pass_on(0, 1)
    begin(1)
    ring_next(2)
    forward_first(1)
    pass_on(1, 3)
    pass_on(1, 1)
    opposite(0)
    opposite(1)
    for rel in (0, 3, 1, 2):
        for half in both:
            forward_second(half, rel)
        if rel == 3:
            ring_next(3)
    for half in both:
        for axis in both:
            four = units.at[0:4, 0, 0, spans[axis][0] : spans[axis][2]]
            pltpu.make_async_copy(four, four, ag_recv.at[axis, half, 8]).wait()
    ring_up(step(z, 4, 8), 3, False).wait_recv()
    ring_down(step(z, 4, 8), 3, False).wait_recv()
    to_mate(step(z, 4, 8), c, 1).start()

    def from_mate_heads(k):
        pltpu.make_async_copy(heads.at[0:4, 0], heads.at[0:4, 0], hp_recv.at[k]).wait()

    for yy in range(4):
        for k in (0, 1):
            total = jnp.zeros((1, 128), F32)
            for xx in range(4):
                for cc in (0, 1):
                    line = units[yy, xx, cc, 256:272, :].astype(F32)[k : k + 1]
                    total = total + line[:, :128] + line[:, 128:]
            factor[yy, k : k + 1] = lax.rsqrt(total * (1.0 / 2048.0) + 1e-5)

    def logits(pair, k, n):
        left = [heads[lax.rem(z + 4 * n + i, 8), :, k].reshape(128, 2048) for i in range(4)]
        left = jnp.concatenate(left, axis=0)
        total = None
        for xx in range(4):
            for cc in (0, 1):
                right = jnp.concatenate(
                    [
                        units[2 * pair + i, xx, cc, 128 * k : 128 * k + 128, :]
                        for i in (0, 1)
                    ],
                    axis=0,
                )
                kk = (xx * 2 + cc) * 256
                term = lax.dot_general(
                    left[:, kk : kk + 256], right, NT, preferred_element_type=F32
                )
                total = term if total is None else total + term
        scale = [factor[2 * pair + i, k : k + 1] for i in (0, 1)]
        return total * jnp.concatenate(scale, axis=1)

    def chunk(n):
        def one_pair(pair, carry):
            tl = logits(pair, 0, n)
            sl = logits(pair, 1, n)
            tm = jnp.max(tl, axis=0, keepdims=True)
            sm = jnp.max(sl, axis=0, keepdims=True)
            if n == 1:
                old = jnp.concatenate([st_send[2 * pair], st_send[2 * pair + 1]], axis=1)
                tm = jnp.maximum(tm, old[0:1])
                sm = jnp.maximum(sm, old[3:4])
            te = jnp.exp(tl - tm)
            ts = jnp.sum(te, axis=0, keepdims=True)
            tw = jnp.sum(te * (tl - sl), axis=0, keepdims=True)
            ss = jnp.sum(jnp.exp(sl - sm), axis=0, keepdims=True)
            if n == 1:
                keep = jnp.exp(old[0:1] - tm)
                ts = ts + old[1:2] * keep
                tw = tw + old[2:3] * keep
                ss = ss + old[4:5] * jnp.exp(old[3:4] - sm)
            zero = jnp.zeros((3, 256), F32)
            table = jnp.concatenate([tm, ts, tw, sm, ss, zero], axis=0)
            st_send[2 * pair] = table[:, :128]
            st_send[2 * pair + 1] = table[:, 128:]
            return carry

        lax.fori_loop(0, 2, one_pair, 0)

    from_mate_heads(0)
    chunk(0)
    from_mate_heads(1)
    chunk(1)

    me = 4 * y + x

    def st_copy(r):
        yy = lax.rem(y + r // 8, 4)
        vv = lax.rem(v + lax.rem(r, 8), 8)
        return remote(
            st_send.at[yy], st_recv.at[c, me], st_ssem.at[0], st_rsem.at[0],
            (z * 4 + yy, vv),
        )

    def send_stats(r, carry):
        st_copy(r).start()
        return carry

    lax.fori_loop(1, 32, send_stats, 0)
    pltpu.make_async_copy(st_send.at[y], st_recv.at[c, me], st_rsem.at[0]).start()

    rw1.wait_send()
    rw2.wait_send()

    for h in (0, 1):

        @pl.when(home != c)
        def _():
            pltpu.make_async_copy(out_rows.at[h], out_rows.at[h], disp_send.at[h]).wait()

        @pl.when(home == c)
        def _():
            most = out_rows.at[h, pl.ds(0, 93)]
            pltpu.make_async_copy(most, most, disp_send.at[h]).wait()

    pltpu.make_async_copy(feats.at[0:3], feats.at[0:3], xag_send.at[0]).wait()
    pltpu.make_async_copy(part_send, part_send, rs_send.at[0]).wait()

    for h in (0, 1):

        @pl.when((home == c) & (c == h))
        def _():
            most = back.at[h, pl.ds(0, 45)]
            pltpu.make_async_copy(most, most, comb_send.at[h]).wait()

        @pl.when(jnp.logical_not((home == c) & (c == h)))
        def _():
            pltpu.make_async_copy(back.at[h], back.at[h], comb_send.at[h]).wait()

    swap.wait_send()
    for axis in both:
        rows_ = slice(spans[axis][0], spans[axis][2])
        for half in both:
            for k, sent in ((0, units.at[0:3, 0, 0, rows_]), (1, units.at[0:3, :, 0, rows_])):
                pltpu.make_async_copy(sent, sent, ag_send.at[axis, half, k]).wait()
    pltpu.make_async_copy(heads.at[0:7, 0], heads.at[0:7, 0], hd_send.at[0]).wait()
    pltpu.make_async_copy(heads.at[:, 0], heads.at[:, 0], hp_send.at[0]).wait()

    pltpu.make_async_copy(st_recv, st_recv, st_rsem.at[0]).wait()
    for cc in (0, 1):
        pieces = st_recv[cc]
        tm, sm = pieces[:, 0], pieces[:, 3]
        tmax = jnp.max(tm, axis=0, keepdims=True)
        smax = jnp.max(sm, axis=0, keepdims=True)
        tk, sk = jnp.exp(tm - tmax), jnp.exp(sm - smax)
        ts = jnp.sum(pieces[:, 1] * tk, axis=0, keepdims=True)
        tw = jnp.sum(pieces[:, 2] * tk, axis=0, keepdims=True)
        ss = jnp.sum(pieces[:, 4] * sk, axis=0, keepdims=True)
        res[cc : cc + 1, :] = tw / ts - tmax - jnp.log(ts) + smax + jnp.log(ss)

    sent = out_rows.at[0, pl.ds(0, 62)]
    cp_out = pltpu.make_async_copy(res, o_ref, load_sem.at[0])
    cp_out.start()
    pltpu.make_async_copy(sent, sent, st_ssem.at[0]).wait()
    cp_out.wait()


def local(
    tokens, teacher_expert, student_expert, priority, expert_in, expert_out,
    teacher_gain, student_gain, teacher_head, student_head,
):
    dma = pltpu.SemaphoreType.DMA
    vm = pltpu.VMEM
    out = pl.pallas_call(
        kernel,
        out_shape=jax.ShapeDtypeStruct((2, 128), F32),
        in_specs=[pl.BlockSpec(memory_space=pl.ANY)] * 10,
        out_specs=pl.BlockSpec(memory_space=pl.ANY),
        scratch_shapes=[
            vm((3, 1, 256), jnp.int32),
            vm((2, 1, 256), F32),
            vm((256, 256), BF),
            vm((2, 96, 8, 128), BF),
            vm((4, 2, 2, 48, 8, 128), BF),
            vm((2, 2048, 1024), BF),
            vm((2048, 2048), BF),
            vm((2, 384, 1024), F32),
            vm((384, 2048), BF),
            vm((2, 6, 192, 256), BF),
            vm((2, 6, 192, 256), BF),
            vm((3, 384, 512), F32),
            vm((4, 384, 512), BF),
            vm((2, 48, 8, 256), BF),
            vm((96, 8, 256), BF),
            vm((272, 256), BF),
            vm((4, 4, 2, 272, 256), BF),
            vm((8, 2, 2, 64, 2048), BF),
            vm((4, 8, 128), F32),
            vm((2, 16, 8, 128), F32),
            vm((512, 768), BF),
            vm((4, 8, 128), F32),
            vm((2, 128), F32),
            dma((6,)),
            dma((2,)), dma((2,)),
            dma((2,)), dma((2,)),
            dma((1,)), dma((2, 6)),
            dma((1,)), dma((2, 6)),
            dma((2,)), dma((1,)),
            dma((1,)), dma((1,)),
            dma((2, 2, 2)), dma((2, 2, 9)),
            dma((1,)), dma((2, 4)),
            dma((1,)), dma((2,)),
            dma((1,)), dma((1,)),
        ],
        compiler_params=pltpu.CompilerParams(
            has_side_effects=True, collective_id=0, vmem_limit_bytes=64 * 1024 * 1024 - 65536
        ),
    )(
        tokens,
        teacher_expert.reshape(1, -1),
        student_expert.reshape(1, -1),
        priority,
        expert_in,
        expert_out,
        teacher_gain.reshape(1, -1),
        student_gain.reshape(1, -1),
        teacher_head,
        student_head,
    )
    return out.reshape(256)


def solution(mesh):
    placed = (
        P("expert", None),
        P("expert", None),
        P("expert", None),
        P("expert", None),
        P("expert", None, "vocab"),
        P("expert", "vocab", None),
        P(),
        P(),
        P(("vocab", "expert"), None),
        P(("vocab", "expert"), None),
    )
    return jax.shard_map(local, mesh=mesh, in_specs=placed, out_specs=P("expert"), check_vma=False)
```

```python
import jax
import jax.numpy as jnp
from jax import lax
from jax.experimental import pallas as pl
from jax.experimental.pallas import tpu as pltpu
from jax.sharding import PartitionSpec as P

MESH = pl.DeviceIdType.MESH
BF = jnp.bfloat16
F32 = jnp.float32
CAP = 24
NT = (((1,), (1,)), ((), ()))


def gelu(v):
    return 0.5 * v * (1.0 + jnp.tanh(0.7978845608028654 * (v + 0.044715 * v * v * v)))


def kernel(
    tok_hbm, te_hbm, se_hbm, pr_hbm, win_hbm, wout_hbm, tg_hbm, sg_hbm, th_hbm, sh_hbm,
    o_ref,
    ids, gains,
    tok, out_rows, feats, w1, w2, acc, hid, part_send, part_recv, own_part, xin,
    back, ret, unit, units, heads, st_send, st_recv, pick, factor, res, square,
    load_sem, w_send, w_recv, disp_send, disp_recv, xag_send, xag_recv,
    rs_send, rs_recv, comb_send, comb_recv, pair_send, pair_recv,
    ag_send, ag_recv, hd_send, hd_recv, hp_send, hp_recv, st_ssem, st_rsem,
):
    e = lax.axis_index("expert")
    v = lax.axis_index("vocab")
    z, y = e // 4, e % 4
    x, c = v // 2, v % 2
    mate = 1 - c
    home = e // 16

    def at(zz, yy, xx, cc):
        return (zz * 4 + yy, xx * 2 + cc)

    def step(a, d, n):
        return lax.rem(a + d + n, n)

    xr, xl, xo = step(x, 1, 4), step(x, -1, 4), step(x, 2, 4)

    def remote(src, dst, ssem, rsem, dev):
        return pltpu.make_async_remote_copy(
            src_ref=src, dst_ref=dst, send_sem=ssem, recv_sem=rsem,
            device_id=dev, device_id_type=MESH,
        )

    cp_tok = pltpu.make_async_copy(
        tok_hbm.at[:, pl.ds(pl.multiple_of(v * 256, 256), 256)], tok, load_sem.at[1]
    )
    cp_ids = [
        pltpu.make_async_copy(src, ids.at[k], load_sem.at[0])
        for k, src in enumerate((te_hbm, se_hbm, pr_hbm))
    ]
    cols = pl.ds(pl.multiple_of(v * 256, 256), 256)
    cp_gains = [
        pltpu.make_async_copy(src.at[:, cols], gains.at[k], load_sem.at[2])
        for k, src in enumerate((tg_hbm, sg_hbm))
    ]
    for cp in cp_ids:
        cp.start()
    cp_tok.start()
    for cp in cp_gains:
        cp.start()
    mine_w2 = pl.ds(pl.multiple_of(c * 1024, 1024), 1024)
    cp_w1 = pltpu.make_async_copy(win_hbm.at[0], w1.at[c], load_sem.at[3])
    cp_w2 = pltpu.make_async_copy(wout_hbm.at[0], w2.at[mine_w2], load_sem.at[4])
    cp_th = pltpu.make_async_copy(th_hbm, heads.at[z, c, 0], load_sem.at[5])
    cp_sh = pltpu.make_async_copy(sh_hbm, heads.at[z, c, 1], load_sem.at[5])
    rw1 = remote(win_hbm.at[0], w1.at[c], w_send.at[0], w_recv.at[0], at(z, y, x, mate))
    rw2 = remote(wout_hbm.at[0], w2.at[mine_w2], w_send.at[1], w_recv.at[1], at(z, y, x, mate))

    barrier = pltpu.get_barrier_semaphore()

    def greet(ee, vv, other):
        def tell():
            pl.semaphore_signal(barrier, inc=1, device_id=(ee, vv), device_id_type=MESH)

        if other is None:
            tell()
        else:
            pl.when(other)(tell)

    far_first = [lax.rem(z + d, 8) for d in (4, 3, 5, 2, 6, 1, 7, 0)]
    x0 = 2 * x
    for k, zz in enumerate(far_first):

        def greet_rows(r, carry):
            ee = zz * 4 + lax.rem(y + 1 + r, 4)
            greet(ee, x0 + home, None if k < 7 else (r < 3) | (home != c))
            return carry

        lax.fori_loop(0, 4, greet_rows, 0)

        @pl.when(zz // 4 == c)
        def _():
            def greet_back(r, carry):
                ee = zz * 4 + lax.rem(y + 1 + r, 4)
                for cc in (0, 1):
                    greet(ee, x0 + cc, None if k < 7 else (r < 3) | (cc != c))
                return carry

            lax.fori_loop(0, 4, greet_back, 0)

    def greet_plane(r, carry):
        for k in range(8):
            vv = lax.rem(v + 1 + k, 8)
            greet(z * 4 + lax.rem(y + 1 + r, 4), vv, None if k < 7 else r < 3)
        return carry

    lax.fori_loop(0, 4, greet_plane, 0)
    greet(step(z, 1, 8) * 4 + y, v, None)
    greet(step(z, -1, 8) * 4 + y, v, None)

    cp_w1.start()
    pltpu.make_async_copy(ids, ids, load_sem.at[0]).wait()

    def spread(row):
        return jnp.broadcast_to(row.astype(F32), (256, 256))

    pj = spread(ids[2])
    pi = pj.T

    def places(expert, lane):
        ej = spread(expert)
        ei = ej.T
        same = ei == ej
        rank_row = jnp.sum(jnp.where(same & (pi < pj), 1.0, 0.0), axis=0, keepdims=True)
        rank_col = jnp.sum(jnp.where(same & (pj < pi), 1.0, 0.0), axis=1, keepdims=True)

        def place(expert, rank):
            return jnp.where(rank < CAP, (2.0 * expert + lane) * CAP + rank, -1.0)

        return place(ej[:1], rank_row), place(ei[:, :1], rank_col)

    t_row, t_col = places(ids[0], 0.0)
    s_row, s_col = places(ids[1], 1.0)
    slot = lax.broadcasted_iota(jnp.int32, (768, 256), 0).astype(F32)
    gather = jnp.where((slot == t_row) | (slot == s_row), 1.0, 0.0).astype(BF)
    lanes = lax.broadcasted_iota(jnp.int32, (256, 768), 1).astype(F32)
    pick[0:256] = jnp.where(lanes == t_col, 1.0, 0.0).astype(BF)
    pick[256:512] = jnp.where(lanes == s_col, 1.0, 0.0).astype(BF)
    cp_tok.wait()
    pltpu.make_async_copy(gains, gains, load_sem.at[2]).wait()
    picked = jnp.dot(gather, tok[...], preferred_element_type=F32)
    out_rows[0] = picked[:, :128].reshape(96, 8, 128).astype(BF)
    out_rows[1] = picked[:, 128:].reshape(96, 8, 128).astype(BF)
    pl.semaphore_wait(barrier, jnp.where(home == c, 95, 97))

    my_slot = pl.ds(3 * lax.rem(e, 16), 3)

    def disp(to, h):
        return remote(
            out_rows.at[h, pl.ds(3 * to, 3)], feats.at[x, c, h, my_slot],
            disp_send.at[h], disp_recv.at[h], (to, x * 2 + home),
        )

    cp_self = [
        pltpu.make_async_copy(
            out_rows.at[h, pl.ds(3 * e, 3)], feats.at[x, c, h, my_slot], disp_recv.at[h]
        )
        for h in (0, 1)
    ]

    for h in (0, 1):

        @pl.when(home == c)
        def _():
            cp_self[h].start()

        @pl.when(home != c)
        def _():
            disp(e, h).start()

        for k, zz in enumerate(far_first):

            def send_rows(r, carry):
                disp(zz * 4 + lax.rem(y + 1 + r, 4), h).start()
                return carry

            lax.fori_loop(0, 3 if k == 7 else 4, send_rows, 0)
    rw1.start()
    rw2.start()
    cp_w2.start()
    cp_th.start()
    cp_sh.start()

    def wait_rows(h):
        here = feats.at[x, :, h]
        remote(
            here, here, disp_send.at[h], disp_recv.at[h], at(z, y, x, mate)
        ).wait_recv()

    def xcopy(xx, cc, h, k, to):
        piece = feats.at[xx, cc, h]
        return remote(piece, piece, xag_send.at[0], xag_recv.at[h, k], at(z, y, to, c))

    for h in (0, 1):
        wait_rows(h)
        xcopy(x, 0, h, 0, xr).start()
        xcopy(x, 1, h, 1, xl).start()
        xcopy(x, 1, h, 2, xr).start()
        xcopy(x, 0, h, 3, xl).start()

    zu, zd = step(z, 1, 8), step(z, -1, 8)
    pltpu.make_async_copy(heads.at[z, c], heads.at[z, c], load_sem.at[5]).wait()

    def ring_up(zz, k, both):
        piece = heads.at[zz, c] if both else heads.at[zz, c, 0]
        return remote(piece, piece, hd_send.at[0], hd_recv.at[0, k], at(zu, y, x, c))

    def ring_down(zz, k, both):
        piece = heads.at[zz, c] if both else heads.at[zz, c, 1]
        return remote(piece, piece, hd_send.at[0], hd_recv.at[1, k], at(zd, y, x, c))

    def to_mate(zz, cc, k):
        piece = heads.at[zz, cc]
        return remote(piece, piece, hp_send.at[0], hp_recv.at[k], at(z, y, x, mate))

    ring_up(z, 0, True).start()
    ring_down(z, 0, True).start()
    to_mate(z, c, 0).start()

    cp_w1.wait()
    rw1.wait_recv()

    def flatten(xx):
        xin[xx] = jnp.concatenate(
            [
                feats[xx, cc, h].astype(F32).reshape(384, 128).astype(BF)
                for cc in (0, 1)
                for h in (0, 1)
            ],
            axis=1,
        )

    def hidden_pass(xs, first, last):
        for xx in xs:
            flatten(xx)

        def body(n, carry):
            cc, m = n // 2, lax.rem(n, 2)
            cols = pl.ds(pl.multiple_of(m * 512, 512), 512)
            total = None if first else acc[cc, :, cols]
            for xx in xs:
                k = pl.ds(pl.multiple_of(xx * 512, 512), 512)
                term = jnp.dot(xin[xx], w1[cc, k, cols], preferred_element_type=F32)
                total = term if total is None else total + term
            if last:
                hid[:, pl.ds(pl.multiple_of(n * 512, 512), 512)] = gelu(total).astype(BF)
            else:
                acc[cc, :, cols] = total
            return carry

        lax.fori_loop(0, 4, body, 0)

    hidden_pass([x], True, False)
    for h in (0, 1):
        xcopy(xl, 0, h, 0, xr).wait_recv()
        xcopy(xl, 0, h, 4, xr).start()
        xcopy(xr, 1, h, 1, xl).wait_recv()
        xcopy(xr, 1, h, 5, xl).start()
        xcopy(xl, 1, h, 2, xr).wait_recv()
        xcopy(xr, 0, h, 3, xl).wait_recv()
    hidden_pass([xl, xr], False, False)
    for h in (0, 1):
        xcopy(xo, 0, h, 4, xr).wait_recv()
        xcopy(xo, 1, h, 5, xl).wait_recv()

    def ring_next(k):
        lo, hi = step(z, -k, 8), step(z, k, 8)
        ring_up(lo, k - 1, True).wait_recv()
        ring_down(hi, k - 1, True).wait_recv()
        ring_up(lo, k, k < 3).start()
        ring_down(hi, k, k < 3).start()
        to_mate(lo, c, 1).start()
        to_mate(hi, c, 0).start()

    hidden_pass([xo], False, True)
    ring_next(1)

    cp_w2.wait()
    rw2.wait_recv()

    def partial(xx):
        cols = pl.ds(pl.multiple_of(xx * 512, 512), 512)
        return jnp.dot(hid[...], w2[:, cols], preferred_element_type=F32)

    def rs(q, k, to):
        return remote(
            part_send.at[q, k], part_recv.at[q, k], rs_send.at[0], rs_recv.at[q, min(k, 2)],
            at(z, y, to, c),
        )

    quarters = range(4)

    def far_sums(q):
        rs(q, 0, xr).start()
        rs(q, 1, xl).start()

    far = partial(xo).astype(BF)
    for q in quarters:
        part_send[q, 0] = far[:192, 128 * q : 128 * q + 128]
        part_send[q, 1] = far[192:, 128 * q : 128 * q + 128]
    far_sums(0)
    own_part[1] = partial(xr)
    for q in quarters:
        part_send[q, 2] = own_part[1, 192:, 128 * q : 128 * q + 128].astype(BF)
    rs(0, 2, xr).start()
    own_part[2] = partial(xl)
    for q in quarters:
        part_send[q, 3] = own_part[2, :192, 128 * q : 128 * q + 128].astype(BF)
    rs(0, 3, xl).start()

    def near_sums(q):
        rs(q, 2, xr).start()
        rs(q, 3, xl).start()

    def merge(q):
        part = slice(128 * q, 128 * q + 128)
        rs(q, 0, xr).wait_recv()
        part_send[q, 4] = (own_part[1, :192, part] + part_recv[q, 0].astype(F32)).astype(BF)
        rs(q, 4, xr).start()
        rs(q, 1, xl).wait_recv()
        part_send[q, 5] = (own_part[2, 192:, part] + part_recv[q, 1].astype(F32)).astype(BF)
        rs(q, 5, xl).start()

    def comb(b, q):
        return remote(
            back.at[q, pl.ds(3 * lax.rem(b, 16), 3)], ret.at[q % 2, pl.ds(3 * e, 3)],
            comb_send.at[q], comb_recv.at[q % 2], (b, x * 2 + q // 2),
        )

    def send_back(q):
        @pl.when((home == c) & (c == q // 2))
        def _():
            pltpu.make_async_copy(
                back.at[q, pl.ds(3 * lax.rem(e, 16), 3)], ret.at[q % 2, pl.ds(3 * e, 3)],
                comb_recv.at[q % 2],
            ).start()

        for zz in far_first:

            @pl.when(zz // 4 == c)
            def _():
                def one(r, carry):
                    b = zz * 4 + lax.rem(y + 1 + r, 4)

                    @pl.when((b != e) | (c != q // 2))
                    def _():
                        comb(b, q).start()

                    return carry

                lax.fori_loop(0, 4, one, 0)

    def collect(q):
        part = slice(128 * q, 128 * q + 128)
        four = part_recv.at[q, 2:6]
        pltpu.make_async_copy(four, four, rs_recv.at[q, 2]).wait()
        for rows_, near, merged in ((slice(0, 192), 3, 4), (slice(192, 384), 2, 5)):
            total = (
                own_part[0, rows_, part]
                + part_recv[q, near].astype(F32)
                + part_recv[q, merged].astype(F32)
            )
            back[q, rows_.start // 8 : rows_.stop // 8] = total.reshape(24, 8, 128).astype(BF)
        send_back(q)

    far_sums(1)
    merge(0)
    near_sums(1)
    far_sums(2)
    own_part[0] = partial(x)
    merge(1)
    collect(0)
    near_sums(2)
    far_sums(3)
    merge(2)
    collect(1)
    near_sums(3)
    merge(3)
    collect(2)
    collect(3)

    def swap(sub):
        return remote(
            unit.at[sub, 0 : 256 + 16 * sub], units.at[y, x, 2 * c + sub, 0 : 256 + 16 * sub],
            pair_send.at[sub], pair_recv.at[sub],
            at(z, y, x, mate),
        )

    def finish(core, sub):
        pltpu.make_async_copy(ret.at[sub], ret.at[sub], comb_recv.at[sub]).wait()
        rows = ret[sub].astype(F32).reshape(768, 128).astype(BF)
        part = slice(128 * sub, 128 * sub + 128)
        stream = tok[:, part].astype(F32)
        kept = units.at[y, x, 2 * core + sub]
        given = unit.at[sub]
        squares = []
        for k in (0, 1):
            branch = jnp.dot(
                pick[256 * k : 256 * k + 256], rows, preferred_element_type=F32
            )
            summed = stream + branch
            scaled = (summed * gains[k, :, part]).astype(BF)
            parts = (scaled[:128], scaled[128:])
            kept[128 * k : 128 * k + 128] = parts[core]
            given[128 * k : 128 * k + 128] = parts[1 - core]
            column = jnp.sum(summed * summed, axis=1, keepdims=True)
            row = jnp.broadcast_to(column, (256, 128)).T[:1]
            if sub == 0:
                square[k : k + 1] = row
            else:
                squares.append(row + square[k : k + 1])
        if sub == 0:
            swap(sub).start()
            return
        line_of = lax.broadcasted_iota(jnp.int32, (16, 128), 0)
        for h, place in ((core, kept), (1 - core, given)):
            table = jnp.zeros((16, 128), F32)
            for k in (0, 1):
                total = squares[k][:, 128 * h : 128 * h + 128]
                top = total.astype(BF).astype(F32)
                for i, line in enumerate((top, total - top)):
                    table = jnp.where(
                        line_of == 2 * k + i, jnp.broadcast_to(line, (16, 128)), table
                    )
            place[256:272] = table.astype(BF)
        swap(sub).start()

    here = (x, y)
    def span(axis, q):
        if (axis + q) % 2 == 0:
            return 0, 64, 128
        return 128, 192, 272 if q % 2 else 256


    def dev_of(along, d):
        p, q = (step(x, d, 4), y) if along == 0 else (x, step(y, d, 4))
        return at(z, q, p, c)

    def hop(axis, q, along, a, b, group, d, ends):
        xx, yy = (a, b) if axis == 0 else (b, a)
        piece = units.at[yy, xx, q, ends[0] : ends[1]]
        return remote(
            piece, piece, ag_send.at[q % 2, min(group // 2, 1)], ag_recv.at[axis, q, group],
            dev_of(along, d),
        )

    def first(axis, q, k, off, d):
        lo, mid, hi = span(axis, q)
        ends = ((lo, hi), (lo, hi), (lo, mid), (mid, hi))[k]
        a = step(here[axis], off, 4)
        return hop(axis, q, axis, a, here[1 - axis], k // 2, d, ends)

    def second(axis, q, rel, off, kind, d):
        a = step(here[axis], rel, 4)
        b = step(here[1 - axis], off, 4)
        lo, _, hi = span(axis, q)
        ends = (lo, hi)
        return hop(axis, q, 1 - axis, a, b, 2 + rel if kind == 0 else 6, d, ends)

    def got(axis, q, group, count):
        lo, _, hi = span(axis, q)
        bulk = units.at[0:count, 0, 0, lo:hi]
        pltpu.make_async_copy(bulk, bulk, ag_recv.at[axis, q, group]).wait()

    both = (0, 1)

    def begin(q):
        @pl.when(c == q // 2)
        def _():
            finish(q // 2, q % 2)

        @pl.when(c != q // 2)
        def _():
            swap(q % 2).wait_recv()

        for axis in both:
            first(axis, q, 0, 0, 1).start()
            first(axis, q, 1, 0, -1).start()
        pass_on(q, 0)

    def forward_first(q):
        for axis in both:
            got(axis, q, 0, 2)
            first(axis, q, 2, -1, 1).start()
            first(axis, q, 3, 1, -1).start()

    def pass_on(q, rel):
        for axis in both:
            second(axis, q, rel, 0, 0, 1).start()
            second(axis, q, rel, 0, 0, -1).start()

    def opposite(q):
        for axis in both:
            got(axis, q, 1, 1)
        pass_on(q, 2)

    def forward_second(q, rel):
        for axis in both:
            got(axis, q, 2 + rel, 2)
            if rel in (0, 1):
                second(axis, q, rel, -1, 1, 1).start()
            else:
                second(axis, q, rel, 1, 1, -1).start()

    def spread_on(q):
        forward_first(q)
        pass_on(q, 3)
        pass_on(q, 1)

    begin(0)
    begin(1)
    spread_on(0)
    begin(2)
    ring_next(2)
    spread_on(1)
    opposite(0)
    begin(3)
    forward_second(0, 0)
    spread_on(2)
    opposite(1)
    forward_second(0, 3)
    forward_second(1, 0)
    forward_second(0, 1)
    spread_on(3)
    opposite(2)
    forward_second(1, 3)
    forward_second(0, 2)
    forward_second(2, 0)
    opposite(3)
    forward_second(1, 1)
    forward_second(1, 2)
    ring_next(3)
    forward_second(2, 3)
    forward_second(3, 0)
    forward_second(2, 1)
    forward_second(3, 3)
    forward_second(2, 2)
    forward_second(3, 1)
    forward_second(3, 2)
    for q in quarters:
        for axis in both:
            got(axis, q, 6, 4)
    ring_up(step(z, 4, 8), 3, False).wait_recv()
    ring_down(step(z, 4, 8), 3, False).wait_recv()
    to_mate(step(z, 4, 8), c, 1).start()

    def from_mate_heads(k):
        pltpu.make_async_copy(heads.at[0:4, 0], heads.at[0:4, 0], hp_recv.at[k]).wait()

    for yy in range(4):
        for k in (0, 1):
            total = jnp.zeros((1, 128), F32)
            for xx in range(4):
                for q in (1, 3):
                    lines = units[yy, xx, q, 256:272, :].astype(F32)
                    total = total + lines[2 * k : 2 * k + 1] + lines[2 * k + 1 : 2 * k + 2]
            factor[yy, k : k + 1] = lax.rsqrt(total * (1.0 / 2048.0) + 1e-5)

    def logits(pair, k, n):
        left = [heads[lax.rem(z + 4 * n + i, 8), :, k].reshape(128, 2048) for i in range(4)]
        left = jnp.concatenate(left, axis=0)
        total = None
        for xx in range(4):
            for cc in (0, 1):
                right = jnp.concatenate(
                    [
                        jnp.concatenate(
                            [
                                units[2 * pair + i, xx, 2 * cc + h, 128 * k : 128 * k + 128, :]
                                for h in (0, 1)
                            ],
                            axis=1,
                        )
                        for i in (0, 1)
                    ],
                    axis=0,
                )
                kk = (xx * 2 + cc) * 256
                term = lax.dot_general(
                    left[:, kk : kk + 256], right, NT, preferred_element_type=F32
                )
                total = term if total is None else total + term
        scale = [factor[2 * pair + i, k : k + 1] for i in (0, 1)]
        return total * jnp.concatenate(scale, axis=1)

    def chunk(n):
        def one_pair(pair, carry):
            tl = logits(pair, 0, n)
            sl = logits(pair, 1, n)
            tm = jnp.max(tl, axis=0, keepdims=True)
            sm = jnp.max(sl, axis=0, keepdims=True)
            if n == 1:
                old = jnp.concatenate([st_send[2 * pair], st_send[2 * pair + 1]], axis=1)
                tm = jnp.maximum(tm, old[0:1])
                sm = jnp.maximum(sm, old[3:4])
            te = jnp.exp(tl - tm)
            ts = jnp.sum(te, axis=0, keepdims=True)
            tw = jnp.sum(te * (tl - sl), axis=0, keepdims=True)
            ss = jnp.sum(jnp.exp(sl - sm), axis=0, keepdims=True)
            if n == 1:
                keep = jnp.exp(old[0:1] - tm)
                ts = ts + old[1:2] * keep
                tw = tw + old[2:3] * keep
                ss = ss + old[4:5] * jnp.exp(old[3:4] - sm)
            zero = jnp.zeros((3, 256), F32)
            table = jnp.concatenate([tm, ts, tw, sm, ss, zero], axis=0)
            st_send[2 * pair] = table[:, :128]
            st_send[2 * pair + 1] = table[:, 128:]
            return carry

        lax.fori_loop(0, 2, one_pair, 0)

    from_mate_heads(0)
    chunk(0)
    from_mate_heads(1)
    chunk(1)

    me = 4 * y + x

    for dy in (2, 1, 3, 0):
        yy = step(y, dy, 4)

        def send_stats(r, carry):
            remote(
                st_send.at[yy], st_recv.at[c, me], st_ssem.at[0], st_rsem.at[0],
                (z * 4 + yy, lax.rem(v + 3 + r, 8)),
            ).start()
            return carry

        if dy:
            lax.fori_loop(0, 8, send_stats, 0)
        else:
            lax.fori_loop(0, 5, send_stats, 0)
            lax.fori_loop(6, 8, send_stats, 0)
    pltpu.make_async_copy(st_send.at[y], st_recv.at[c, me], st_rsem.at[0]).start()

    rw1.wait_send()
    rw2.wait_send()

    for h in (0, 1):

        @pl.when(home != c)
        def _():
            pltpu.make_async_copy(out_rows.at[h], out_rows.at[h], disp_send.at[h]).wait()

        @pl.when(home == c)
        def _():
            most = out_rows.at[h, pl.ds(0, 93)]
            pltpu.make_async_copy(most, most, disp_send.at[h]).wait()

    pltpu.make_async_copy(feats.at[0:3], feats.at[0:3], xag_send.at[0]).wait()
    pltpu.make_async_copy(part_send, part_send, rs_send.at[0]).wait()

    for q in quarters:

        @pl.when((home == c) & (c == q // 2))
        def _():
            most = back.at[q, pl.ds(0, 45)]
            pltpu.make_async_copy(most, most, comb_send.at[q]).wait()

        @pl.when(jnp.logical_not((home == c) & (c == q // 2)))
        def _():
            pltpu.make_async_copy(back.at[q], back.at[q], comb_send.at[q]).wait()

    for sub in (0, 1):
        swap(sub).wait_send()
    for sub, rows_ in ((0, 256), (1, 272)):
        for k, sent in (
            (0, units.at[0:3, 0, 0:2, 0:rows_]),
            (1, units.at[0:3, :, 0:2, 0:rows_]),
        ):
            pltpu.make_async_copy(sent, sent, ag_send.at[sub, k]).wait()
    pltpu.make_async_copy(heads.at[0:7, 0], heads.at[0:7, 0], hd_send.at[0]).wait()
    pltpu.make_async_copy(heads.at[:, 0], heads.at[:, 0], hp_send.at[0]).wait()

    pltpu.make_async_copy(st_recv, st_recv, st_rsem.at[0]).wait()
    for cc in (0, 1):
        pieces = st_recv[cc]
        tm, sm = pieces[:, 0], pieces[:, 3]
        tmax = jnp.max(tm, axis=0, keepdims=True)
        smax = jnp.max(sm, axis=0, keepdims=True)
        tk, sk = jnp.exp(tm - tmax), jnp.exp(sm - smax)
        ts = jnp.sum(pieces[:, 1] * tk, axis=0, keepdims=True)
        tw = jnp.sum(pieces[:, 2] * tk, axis=0, keepdims=True)
        ss = jnp.sum(pieces[:, 4] * sk, axis=0, keepdims=True)
        res[cc : cc + 1, :] = tw / ts - tmax - jnp.log(ts) + smax + jnp.log(ss)

    sent = out_rows.at[0, pl.ds(0, 62)]
    cp_out = pltpu.make_async_copy(res, o_ref, load_sem.at[0])
    cp_out.start()
    pltpu.make_async_copy(sent, sent, st_ssem.at[0]).wait()
    cp_out.wait()


def local(
    tokens, teacher_expert, student_expert, priority, expert_in, expert_out,
    teacher_gain, student_gain, teacher_head, student_head,
):
    dma = pltpu.SemaphoreType.DMA
    vm = pltpu.VMEM
    out = pl.pallas_call(
        kernel,
        out_shape=jax.ShapeDtypeStruct((2, 128), F32),
        in_specs=[pl.BlockSpec(memory_space=pl.ANY)] * 10,
        out_specs=pl.BlockSpec(memory_space=pl.ANY),
        scratch_shapes=[
            vm((3, 1, 256), jnp.int32),
            vm((2, 1, 256), F32),
            vm((256, 256), BF),
            vm((2, 96, 8, 128), BF),
            vm((4, 2, 2, 48, 8, 128), BF),
            vm((2, 2048, 1024), BF),
            vm((2048, 2048), BF),
            vm((2, 384, 1024), F32),
            vm((384, 2048), BF),
            vm((4, 6, 192, 128), BF),
            vm((4, 6, 192, 128), BF),
            vm((3, 384, 512), F32),
            vm((4, 384, 512), BF),
            vm((4, 48, 8, 128), BF),
            vm((2, 96, 8, 128), BF),
            vm((2, 272, 128), BF),
            vm((4, 4, 4, 272, 128), BF),
            vm((8, 2, 2, 64, 2048), BF),
            vm((4, 8, 128), F32),
            vm((2, 16, 8, 128), F32),
            vm((512, 768), BF),
            vm((4, 8, 128), F32),
            vm((2, 128), F32),
            vm((8, 256), F32),
            dma((6,)),
            dma((2,)), dma((2,)),
            dma((2,)), dma((2,)),
            dma((1,)), dma((2, 6)),
            dma((1,)), dma((4, 3)),
            dma((4,)), dma((2,)),
            dma((2,)), dma((2,)),
            dma((2, 2)), dma((2, 4, 7)),
            dma((1,)), dma((2, 4)),
            dma((1,)), dma((2,)),
            dma((1,)), dma((1,)),
        ],
        compiler_params=pltpu.CompilerParams(
            has_side_effects=True, collective_id=0, vmem_limit_bytes=64 * 1024 * 1024 - 65536
        ),
    )(
        tokens,
        teacher_expert.reshape(1, -1),
        student_expert.reshape(1, -1),
        priority,
        expert_in,
        expert_out,
        teacher_gain.reshape(1, -1),
        student_gain.reshape(1, -1),
        teacher_head,
        student_head,
    )
    return out.reshape(256)


def solution(mesh):
    placed = (
        P("expert", None),
        P("expert", None),
        P("expert", None),
        P("expert", None),
        P("expert", None, "vocab"),
        P("expert", "vocab", None),
        P(),
        P(),
        P(("vocab", "expert"), None),
        P(("vocab", "expert"), None),
    )
    return jax.shard_map(local, mesh=mesh, in_specs=placed, out_specs=P("expert"), check_vma=False)
```

```python
import jax
import jax.numpy as jnp
from jax import lax
from jax.experimental import pallas as pl
from jax.experimental.pallas import tpu as pltpu
from jax.sharding import PartitionSpec as P

MESH = pl.DeviceIdType.MESH
BF = jnp.bfloat16
F32 = jnp.float32
CAP = 24
NT = (((1,), (1,)), ((), ()))


def gelu(v):
    return 0.5 * v * (1.0 + jnp.tanh(0.7978845608028654 * (v + 0.044715 * v * v * v)))


def kernel(
    tok_hbm, te_hbm, se_hbm, pr_hbm, win_hbm, wout_hbm, tg_hbm, sg_hbm, th_hbm, sh_hbm,
    o_ref,
    ids, gains,
    tok, out_rows, feats, w1, w2, acc, hid, part_send, part_recv, own_part, xin,
    back, ret, unit, units, heads, st_send, st_recv, pick, factor, res, square,
    load_sem, w_send, w_recv, disp_send, disp_recv, xag_send, xag_recv,
    rs_send, rs_recv, comb_send, comb_recv, pair_send, pair_recv,
    ag_send, ag_recv, hd_send, hd_recv, hp_send, hp_recv, st_ssem, st_rsem,
):
    e = lax.axis_index("expert")
    v = lax.axis_index("vocab")
    z, y = e // 4, e % 4
    x, c = v // 2, v % 2
    mate = 1 - c
    home = e // 16

    def at(zz, yy, xx, cc):
        return (zz * 4 + yy, xx * 2 + cc)

    def step(a, d, n):
        return lax.rem(a + d + n, n)

    xr, xl, xo = step(x, 1, 4), step(x, -1, 4), step(x, 2, 4)

    def remote(src, dst, ssem, rsem, dev):
        return pltpu.make_async_remote_copy(
            src_ref=src, dst_ref=dst, send_sem=ssem, recv_sem=rsem,
            device_id=dev, device_id_type=MESH,
        )

    cp_tok = pltpu.make_async_copy(
        tok_hbm.at[:, pl.ds(pl.multiple_of(v * 256, 256), 256)], tok, load_sem.at[1]
    )
    cp_ids = [
        pltpu.make_async_copy(src, ids.at[k], load_sem.at[0])
        for k, src in enumerate((te_hbm, se_hbm, pr_hbm))
    ]
    cols = pl.ds(pl.multiple_of(v * 256, 256), 256)
    cp_gains = [
        pltpu.make_async_copy(src.at[:, cols], gains.at[k], load_sem.at[2])
        for k, src in enumerate((tg_hbm, sg_hbm))
    ]
    for cp in cp_ids:
        cp.start()
    cp_tok.start()
    for cp in cp_gains:
        cp.start()
    mine_w2 = pl.ds(pl.multiple_of(c * 1024, 1024), 1024)
    cp_w1 = pltpu.make_async_copy(win_hbm.at[0], w1.at[c], load_sem.at[3])
    cp_w2 = pltpu.make_async_copy(wout_hbm.at[0], w2.at[mine_w2], load_sem.at[4])
    cp_th = pltpu.make_async_copy(th_hbm, heads.at[z, c, 0], load_sem.at[5])
    cp_sh = pltpu.make_async_copy(sh_hbm, heads.at[z, c, 1], load_sem.at[5])
    rw1 = remote(win_hbm.at[0], w1.at[c], w_send.at[0], w_recv.at[0], at(z, y, x, mate))
    rw2 = remote(wout_hbm.at[0], w2.at[mine_w2], w_send.at[1], w_recv.at[1], at(z, y, x, mate))

    barrier = pltpu.get_barrier_semaphore()

    def greet(ee, vv, other):
        def tell():
            pl.semaphore_signal(barrier, inc=1, device_id=(ee, vv), device_id_type=MESH)

        if other is None:
            tell()
        else:
            pl.when(other)(tell)

    far_first = [lax.rem(z + d, 8) for d in (4, 3, 5, 2, 6, 1, 7, 0)]
    x0 = 2 * x
    for k, zz in enumerate(far_first):

        def greet_rows(r, carry):
            ee = zz * 4 + lax.rem(y + 1 + r, 4)
            greet(ee, x0 + home, None if k < 7 else (r < 3) | (home != c))
            return carry

        lax.fori_loop(0, 4, greet_rows, 0)

        @pl.when(zz // 4 == c)
        def _():
            def greet_back(r, carry):
                ee = zz * 4 + lax.rem(y + 1 + r, 4)
                for cc in (0, 1):
                    greet(ee, x0 + cc, None if k < 7 else (r < 3) | (cc != c))
                return carry

            lax.fori_loop(0, 4, greet_back, 0)

    def greet_plane(r, carry):
        for k in range(8):
            vv = lax.rem(v + 1 + k, 8)
            greet(z * 4 + lax.rem(y + 1 + r, 4), vv, None if k < 7 else r < 3)
        return carry

    lax.fori_loop(0, 4, greet_plane, 0)
    greet(step(z, 1, 8) * 4 + y, v, None)
    greet(step(z, -1, 8) * 4 + y, v, None)

    cp_w1.start()
    pltpu.make_async_copy(ids, ids, load_sem.at[0]).wait()

    def spread(row):
        return jnp.broadcast_to(row.astype(F32), (256, 256))

    pj = spread(ids[2])
    pi = pj.T

    def places(expert, lane):
        ej = spread(expert)
        ei = ej.T
        same = ei == ej
        rank_row = jnp.sum(jnp.where(same & (pi < pj), 1.0, 0.0), axis=0, keepdims=True)
        rank_col = jnp.sum(jnp.where(same & (pj < pi), 1.0, 0.0), axis=1, keepdims=True)

        def place(expert, rank):
            return jnp.where(rank < CAP, (2.0 * expert + lane) * CAP + rank, -1.0)

        return place(ej[:1], rank_row), place(ei[:, :1], rank_col)

    t_row, t_col = places(ids[0], 0.0)
    s_row, s_col = places(ids[1], 1.0)
    slot = lax.broadcasted_iota(jnp.int32, (768, 256), 0).astype(F32)
    gather = jnp.where((slot == t_row) | (slot == s_row), 1.0, 0.0).astype(BF)
    lanes = lax.broadcasted_iota(jnp.int32, (256, 768), 1).astype(F32)
    pick[0:256] = jnp.where(lanes == t_col, 1.0, 0.0).astype(BF)
    pick[256:512] = jnp.where(lanes == s_col, 1.0, 0.0).astype(BF)
    cp_tok.wait()
    pltpu.make_async_copy(gains, gains, load_sem.at[2]).wait()
    picked = jnp.dot(gather, tok[...], preferred_element_type=F32)
    out_rows[0] = picked[:, :128].reshape(96, 8, 128).astype(BF)
    out_rows[1] = picked[:, 128:].reshape(96, 8, 128).astype(BF)
    pl.semaphore_wait(barrier, jnp.where(home == c, 95, 97))

    my_slot = pl.ds(3 * lax.rem(e, 16), 3)

    def disp(to, h):
        return remote(
            out_rows.at[h, pl.ds(3 * to, 3)], feats.at[x, c, h, my_slot],
            disp_send.at[h], disp_recv.at[h], (to, x * 2 + home),
        )

    cp_self = [
        pltpu.make_async_copy(
            out_rows.at[h, pl.ds(3 * e, 3)], feats.at[x, c, h, my_slot], disp_recv.at[h]
        )
        for h in (0, 1)
    ]

    for h in (0, 1):

        @pl.when(home == c)
        def _():
            cp_self[h].start()

        @pl.when(home != c)
        def _():
            disp(e, h).start()

        for k, zz in enumerate(far_first):

            def send_rows(r, carry):
                disp(zz * 4 + lax.rem(y + 1 + r, 4), h).start()
                return carry

            lax.fori_loop(0, 3 if k == 7 else 4, send_rows, 0)
    rw1.start()
    rw2.start()
    cp_w2.start()
    cp_th.start()
    cp_sh.start()

    def wait_rows(h):
        here = feats.at[x, :, h]
        remote(
            here, here, disp_send.at[h], disp_recv.at[h], at(z, y, x, mate)
        ).wait_recv()

    def xcopy(xx, cc, h, k, to):
        piece = feats.at[xx, cc, h]
        return remote(piece, piece, xag_send.at[0], xag_recv.at[h, k], at(z, y, to, c))

    for h in (0, 1):
        wait_rows(h)
        xcopy(x, 0, h, 0, xr).start()
        xcopy(x, 1, h, 1, xl).start()
        xcopy(x, 1, h, 2, xr).start()
        xcopy(x, 0, h, 3, xl).start()

    zu, zd = step(z, 1, 8), step(z, -1, 8)
    pltpu.make_async_copy(heads.at[z, c], heads.at[z, c], load_sem.at[5]).wait()

    def ring_up(zz, k, both):
        piece = heads.at[zz, c] if both else heads.at[zz, c, 0]
        return remote(piece, piece, hd_send.at[0], hd_recv.at[0, k], at(zu, y, x, c))

    def ring_down(zz, k, both):
        piece = heads.at[zz, c] if both else heads.at[zz, c, 1]
        return remote(piece, piece, hd_send.at[0], hd_recv.at[1, k], at(zd, y, x, c))

    def to_mate(zz, cc, k):
        piece = heads.at[zz, cc]
        return remote(piece, piece, hp_send.at[0], hp_recv.at[k], at(z, y, x, mate))

    ring_up(z, 0, True).start()
    ring_down(z, 0, True).start()
    to_mate(z, c, 0).start()

    cp_w1.wait()
    rw1.wait_recv()

    def flatten(xx):
        xin[xx] = jnp.concatenate(
            [
                feats[xx, cc, h].astype(F32).reshape(384, 128).astype(BF)
                for cc in (0, 1)
                for h in (0, 1)
            ],
            axis=1,
        )

    def hidden_pass(xs, first, last):
        for xx in xs:
            flatten(xx)

        def body(n, carry):
            cc, m = n // 2, lax.rem(n, 2)
            cols = pl.ds(pl.multiple_of(m * 512, 512), 512)
            total = None if first else acc[cc, :, cols]
            for xx in xs:
                k = pl.ds(pl.multiple_of(xx * 512, 512), 512)
                term = jnp.dot(xin[xx], w1[cc, k, cols], preferred_element_type=F32)
                total = term if total is None else total + term
            if last:
                hid[:, pl.ds(pl.multiple_of(n * 512, 512), 512)] = gelu(total).astype(BF)
            else:
                acc[cc, :, cols] = total
            return carry

        lax.fori_loop(0, 4, body, 0)

    hidden_pass([x], True, False)
    for h in (0, 1):
        xcopy(xl, 0, h, 0, xr).wait_recv()
        xcopy(xl, 0, h, 4, xr).start()
        xcopy(xr, 1, h, 1, xl).wait_recv()
        xcopy(xr, 1, h, 5, xl).start()
        xcopy(xl, 1, h, 2, xr).wait_recv()
        xcopy(xr, 0, h, 3, xl).wait_recv()
    hidden_pass([xl, xr], False, False)
    for h in (0, 1):
        xcopy(xo, 0, h, 4, xr).wait_recv()
        xcopy(xo, 1, h, 5, xl).wait_recv()

    def ring_next(k):
        lo, hi = step(z, -k, 8), step(z, k, 8)
        ring_up(lo, k - 1, True).wait_recv()
        ring_down(hi, k - 1, True).wait_recv()
        ring_up(lo, k, k < 3).start()
        ring_down(hi, k, k < 3).start()
        to_mate(lo, c, 1).start()
        to_mate(hi, c, 0).start()

    hidden_pass([xo], False, True)
    ring_next(1)

    cp_w2.wait()
    rw2.wait_recv()

    def partial(xx):
        cols = pl.ds(pl.multiple_of(xx * 512, 512), 512)
        return jnp.dot(hid[...], w2[:, cols], preferred_element_type=F32)

    def rs(q, k, to):
        return remote(
            part_send.at[q, k], part_recv.at[q, k], rs_send.at[0], rs_recv.at[q, min(k, 2)],
            at(z, y, to, c),
        )

    quarters = range(4)

    def far_sums(q):
        rs(q, 0, xr).start()
        rs(q, 1, xl).start()

    far = partial(xo).astype(BF)
    for q in quarters:
        part_send[q, 0] = far[:192, 128 * q : 128 * q + 128]
        part_send[q, 1] = far[192:, 128 * q : 128 * q + 128]
    far_sums(0)
    own_part[1] = partial(xr)
    for q in quarters:
        part_send[q, 2] = own_part[1, 192:, 128 * q : 128 * q + 128].astype(BF)
    rs(0, 2, xr).start()
    own_part[2] = partial(xl)
    for q in quarters:
        part_send[q, 3] = own_part[2, :192, 128 * q : 128 * q + 128].astype(BF)
    rs(0, 3, xl).start()

    def near_sums(q):
        rs(q, 2, xr).start()
        rs(q, 3, xl).start()

    def merge(q):
        part = slice(128 * q, 128 * q + 128)
        rs(q, 0, xr).wait_recv()
        part_send[q, 4] = (own_part[1, :192, part] + part_recv[q, 0].astype(F32)).astype(BF)
        rs(q, 4, xr).start()
        rs(q, 1, xl).wait_recv()
        part_send[q, 5] = (own_part[2, 192:, part] + part_recv[q, 1].astype(F32)).astype(BF)
        rs(q, 5, xl).start()

    def comb(b, q):
        return remote(
            back.at[q, pl.ds(3 * lax.rem(b, 16), 3)], ret.at[q % 2, pl.ds(3 * e, 3)],
            comb_send.at[q], comb_recv.at[q % 2], (b, x * 2 + q // 2),
        )

    def send_back(q):
        @pl.when((home == c) & (c == q // 2))
        def _():
            pltpu.make_async_copy(
                back.at[q, pl.ds(3 * lax.rem(e, 16), 3)], ret.at[q % 2, pl.ds(3 * e, 3)],
                comb_recv.at[q % 2],
            ).start()

        for zz in far_first:

            @pl.when(zz // 4 == c)
            def _():
                def one(r, carry):
                    b = zz * 4 + lax.rem(y + 1 + r, 4)

                    @pl.when((b != e) | (c != q // 2))
                    def _():
                        comb(b, q).start()

                    return carry

                lax.fori_loop(0, 4, one, 0)

    def collect(q):
        part = slice(128 * q, 128 * q + 128)
        four = part_recv.at[q, 2:6]
        pltpu.make_async_copy(four, four, rs_recv.at[q, 2]).wait()
        for rows_, near, merged in ((slice(0, 192), 3, 4), (slice(192, 384), 2, 5)):
            total = (
                own_part[0, rows_, part]
                + part_recv[q, near].astype(F32)
                + part_recv[q, merged].astype(F32)
            )
            back[q, rows_.start // 8 : rows_.stop // 8] = total.reshape(24, 8, 128).astype(BF)
        send_back(q)

    far_sums(1)
    merge(0)
    near_sums(1)
    far_sums(2)
    own_part[0] = partial(x)
    merge(1)
    collect(0)
    near_sums(2)
    far_sums(3)
    merge(2)
    collect(1)
    near_sums(3)
    merge(3)
    collect(2)
    collect(3)

    def swap(sub):
        return remote(
            unit.at[sub, 0 : 256 + 16 * sub], units.at[y, x, 2 * c + sub, 0 : 256 + 16 * sub],
            pair_send.at[sub], pair_recv.at[sub],
            at(z, y, x, mate),
        )

    def finish(core, sub):
        pltpu.make_async_copy(ret.at[sub], ret.at[sub], comb_recv.at[sub]).wait()
        rows = ret[sub].astype(F32).reshape(768, 128).astype(BF)
        part = slice(128 * sub, 128 * sub + 128)
        stream = tok[:, part].astype(F32)
        kept = units.at[y, x, 2 * core + sub]
        given = unit.at[sub]
        squares = []
        for k in (0, 1):
            branch = jnp.dot(
                pick[256 * k : 256 * k + 256], rows, preferred_element_type=F32
            )
            summed = stream + branch
            scaled = (summed * gains[k, :, part]).astype(BF)
            parts = (scaled[:128], scaled[128:])
            kept[128 * k : 128 * k + 128] = parts[core]
            given[128 * k : 128 * k + 128] = parts[1 - core]
            column = jnp.sum(summed * summed, axis=1, keepdims=True)
            row = jnp.broadcast_to(column, (256, 128)).T[:1]
            if sub == 0:
                square[k : k + 1] = row
            else:
                squares.append(row + square[k : k + 1])
        if sub == 0:
            swap(sub).start()
            return
        line_of = lax.broadcasted_iota(jnp.int32, (16, 128), 0)
        for h, place in ((core, kept), (1 - core, given)):
            table = jnp.zeros((16, 128), F32)
            for k in (0, 1):
                total = squares[k][:, 128 * h : 128 * h + 128]
                top = total.astype(BF).astype(F32)
                for i, line in enumerate((top, total - top)):
                    table = jnp.where(
                        line_of == 2 * k + i, jnp.broadcast_to(line, (16, 128)), table
                    )
            place[256:272] = table.astype(BF)
        swap(sub).start()

    here = (x, y)
    def span(axis, q):
        if (axis + q) % 2 == 0:
            return 0, 64, 128
        return 128, 192, 272 if q % 2 else 256


    def dev_of(along, d):
        p, q = (step(x, d, 4), y) if along == 0 else (x, step(y, d, 4))
        return at(z, q, p, c)

    def hop(axis, q, along, a, b, group, d, ends):
        xx, yy = (a, b) if axis == 0 else (b, a)
        piece = units.at[yy, xx, q, ends[0] : ends[1]]
        return remote(
            piece, piece, ag_send.at[q % 2, min(group // 2, 1)], ag_recv.at[axis, q, group],
            dev_of(along, d),
        )

    def first(axis, q, k, off, d):
        lo, mid, hi = span(axis, q)
        ends = ((lo, hi), (lo, hi), (lo, mid), (mid, hi))[k]
        a = step(here[axis], off, 4)
        return hop(axis, q, axis, a, here[1 - axis], k // 2, d, ends)

    def second(axis, q, rel, off, kind, d):
        a = step(here[axis], rel, 4)
        b = step(here[1 - axis], off, 4)
        lo, _, hi = span(axis, q)
        ends = (lo, hi)
        return hop(axis, q, 1 - axis, a, b, 2 + rel if kind == 0 else 6, d, ends)

    def got(axis, q, group, count):
        lo, _, hi = span(axis, q)
        bulk = units.at[0:count, 0, 0, lo:hi]
        pltpu.make_async_copy(bulk, bulk, ag_recv.at[axis, q, group]).wait()

    both = (0, 1)

    def begin(q):
        @pl.when(c == q // 2)
        def _():
            finish(q // 2, q % 2)

        @pl.when(c != q // 2)
        def _():
            swap(q % 2).wait_recv()

        for axis in both:
            first(axis, q, 0, 0, 1).start()
            first(axis, q, 1, 0, -1).start()
        pass_on(q, 0)

    def forward_first(q):
        for axis in both:
            got(axis, q, 0, 2)
            first(axis, q, 2, -1, 1).start()
            first(axis, q, 3, 1, -1).start()

    def pass_on(q, rel):
        for axis in both:
            second(axis, q, rel, 0, 0, 1).start()
            second(axis, q, rel, 0, 0, -1).start()

    def opposite(q):
        for axis in both:
            got(axis, q, 1, 1)
        pass_on(q, 2)

    def forward_second(q, rel):
        for axis in both:
            got(axis, q, 2 + rel, 2)
            if rel in (0, 1):
                second(axis, q, rel, -1, 1, 1).start()
            else:
                second(axis, q, rel, 1, 1, -1).start()

    def spread_on(q):
        forward_first(q)
        pass_on(q, 3)
        pass_on(q, 1)

    begin(0)
    begin(1)
    spread_on(0)
    begin(2)
    ring_next(2)
    spread_on(1)
    opposite(0)
    begin(3)
    forward_second(0, 0)
    spread_on(2)
    opposite(1)
    forward_second(0, 3)
    forward_second(1, 0)
    forward_second(0, 1)
    spread_on(3)
    opposite(2)
    forward_second(1, 3)
    forward_second(0, 2)
    forward_second(2, 0)
    opposite(3)
    forward_second(1, 1)
    forward_second(1, 2)
    ring_next(3)
    forward_second(2, 3)
    forward_second(3, 0)
    forward_second(2, 1)
    forward_second(3, 3)
    forward_second(2, 2)
    forward_second(3, 1)
    forward_second(3, 2)
    for q in quarters:
        got(1, q, 6, 4)
    def from_mate_heads(k):
        pltpu.make_async_copy(heads.at[0:4, 0], heads.at[0:4, 0], hp_recv.at[k]).wait()

    def factors(pair):
        for i in (0, 1):
            for k in (0, 1):
                total = jnp.zeros((1, 128), F32)
                for xx in range(4):
                    for q in (1, 3):
                        lines = units[2 * pair + i, xx, q, 256:272, :].astype(F32)
                        total = total + lines[2 * k : 2 * k + 1] + lines[2 * k + 1 : 2 * k + 2]
                factor[2 * pair + i, k : k + 1] = lax.rsqrt(total * (1.0 / 2048.0) + 1e-5)

    def logits(pair, k, n):
        left = [heads[lax.rem(z + 4 * n + i, 8), :, k].reshape(128, 2048) for i in range(4)]
        left = jnp.concatenate(left, axis=0)
        total = None
        for xx in range(4):
            for cc in (0, 1):
                right = jnp.concatenate(
                    [
                        jnp.concatenate(
                            [
                                units[2 * pair + i, xx, 2 * cc + h, 128 * k : 128 * k + 128, :]
                                for h in (0, 1)
                            ],
                            axis=1,
                        )
                        for i in (0, 1)
                    ],
                    axis=0,
                )
                kk = (xx * 2 + cc) * 256
                term = lax.dot_general(
                    left[:, kk : kk + 256], right, NT, preferred_element_type=F32
                )
                total = term if total is None else total + term
        scale = [factor[2 * pair + i, k : k + 1] for i in (0, 1)]
        return total * jnp.concatenate(scale, axis=1)

    def one_pair(pair, n):
        tl = logits(pair, 0, n)
        sl = logits(pair, 1, n)
        tm = jnp.max(tl, axis=0, keepdims=True)
        sm = jnp.max(sl, axis=0, keepdims=True)
        if n == 1:
            old = jnp.concatenate([st_send[2 * pair], st_send[2 * pair + 1]], axis=1)
            tm = jnp.maximum(tm, old[0:1])
            sm = jnp.maximum(sm, old[3:4])
        te = jnp.exp(tl - tm)
        ts = jnp.sum(te, axis=0, keepdims=True)
        tw = jnp.sum(te * (tl - sl), axis=0, keepdims=True)
        ss = jnp.sum(jnp.exp(sl - sm), axis=0, keepdims=True)
        if n == 1:
            keep = jnp.exp(old[0:1] - tm)
            ts = ts + old[1:2] * keep
            tw = tw + old[2:3] * keep
            ss = ss + old[4:5] * jnp.exp(old[3:4] - sm)
        zero = jnp.zeros((3, 256), F32)
        table = jnp.concatenate([tm, ts, tw, sm, ss, zero], axis=0)
        st_send[2 * pair] = table[:, :128]
        st_send[2 * pair + 1] = table[:, 128:]

    near_pair = y // 2
    from_mate_heads(0)
    factors(near_pair)
    one_pair(near_pair, 0)
    for q in quarters:
        got(0, q, 6, 4)
    for k, arrived in enumerate((ring_up, ring_down)):
        arrived(step(z, 4, 8), 3, False).wait_recv()
        piece = heads.at[step(z, 4, 8), c, k]
        remote(piece, piece, hp_send.at[0], hp_recv.at[1], at(z, y, x, mate)).start()
    factors(1 - near_pair)
    one_pair(1 - near_pair, 0)
    from_mate_heads(1)

    def second_chunk(pair, carry):
        one_pair(pair, 1)
        return carry

    lax.fori_loop(0, 2, second_chunk, 0)

    me = 4 * y + x

    for dy in (2, 1, 3, 0):
        yy = step(y, dy, 4)

        def send_stats(r, carry):
            remote(
                st_send.at[yy], st_recv.at[c, me], st_ssem.at[0], st_rsem.at[0],
                (z * 4 + yy, lax.rem(v + 3 + r, 8)),
            ).start()
            return carry

        if dy:
            lax.fori_loop(0, 8, send_stats, 0)
        else:
            lax.fori_loop(0, 5, send_stats, 0)
            lax.fori_loop(6, 8, send_stats, 0)
    pltpu.make_async_copy(st_send.at[y], st_recv.at[c, me], st_rsem.at[0]).start()

    rw1.wait_send()
    rw2.wait_send()

    for h in (0, 1):

        @pl.when(home != c)
        def _():
            pltpu.make_async_copy(out_rows.at[h], out_rows.at[h], disp_send.at[h]).wait()

        @pl.when(home == c)
        def _():
            most = out_rows.at[h, pl.ds(0, 93)]
            pltpu.make_async_copy(most, most, disp_send.at[h]).wait()

    pltpu.make_async_copy(feats.at[0:3], feats.at[0:3], xag_send.at[0]).wait()
    pltpu.make_async_copy(part_send, part_send, rs_send.at[0]).wait()

    for q in quarters:

        @pl.when((home == c) & (c == q // 2))
        def _():
            most = back.at[q, pl.ds(0, 45)]
            pltpu.make_async_copy(most, most, comb_send.at[q]).wait()

        @pl.when(jnp.logical_not((home == c) & (c == q // 2)))
        def _():
            pltpu.make_async_copy(back.at[q], back.at[q], comb_send.at[q]).wait()

    for sub in (0, 1):
        swap(sub).wait_send()
    for sub, rows_ in ((0, 256), (1, 272)):
        for k, sent in (
            (0, units.at[0:3, 0, 0:2, 0:rows_]),
            (1, units.at[0:3, :, 0:2, 0:rows_]),
        ):
            pltpu.make_async_copy(sent, sent, ag_send.at[sub, k]).wait()
    pltpu.make_async_copy(heads.at[0:7, 0], heads.at[0:7, 0], hd_send.at[0]).wait()
    pltpu.make_async_copy(heads.at[:, 0], heads.at[:, 0], hp_send.at[0]).wait()

    pltpu.make_async_copy(st_recv, st_recv, st_rsem.at[0]).wait()
    for cc in (0, 1):
        pieces = st_recv[cc]
        tm, sm = pieces[:, 0], pieces[:, 3]
        tmax = jnp.max(tm, axis=0, keepdims=True)
        smax = jnp.max(sm, axis=0, keepdims=True)
        tk, sk = jnp.exp(tm - tmax), jnp.exp(sm - smax)
        ts = jnp.sum(pieces[:, 1] * tk, axis=0, keepdims=True)
        tw = jnp.sum(pieces[:, 2] * tk, axis=0, keepdims=True)
        ss = jnp.sum(pieces[:, 4] * sk, axis=0, keepdims=True)
        res[cc : cc + 1, :] = tw / ts - tmax - jnp.log(ts) + smax + jnp.log(ss)

    sent = out_rows.at[0, pl.ds(0, 62)]
    cp_out = pltpu.make_async_copy(res, o_ref, load_sem.at[0])
    cp_out.start()
    pltpu.make_async_copy(sent, sent, st_ssem.at[0]).wait()
    cp_out.wait()


def local(
    tokens, teacher_expert, student_expert, priority, expert_in, expert_out,
    teacher_gain, student_gain, teacher_head, student_head,
):
    dma = pltpu.SemaphoreType.DMA
    vm = pltpu.VMEM
    out = pl.pallas_call(
        kernel,
        out_shape=jax.ShapeDtypeStruct((2, 128), F32),
        in_specs=[pl.BlockSpec(memory_space=pl.ANY)] * 10,
        out_specs=pl.BlockSpec(memory_space=pl.ANY),
        scratch_shapes=[
            vm((3, 1, 256), jnp.int32),
            vm((2, 1, 256), F32),
            vm((256, 256), BF),
            vm((2, 96, 8, 128), BF),
            vm((4, 2, 2, 48, 8, 128), BF),
            vm((2, 2048, 1024), BF),
            vm((2048, 2048), BF),
            vm((2, 384, 1024), F32),
            vm((384, 2048), BF),
            vm((4, 6, 192, 128), BF),
            vm((4, 6, 192, 128), BF),
            vm((3, 384, 512), F32),
            vm((4, 384, 512), BF),
            vm((4, 48, 8, 128), BF),
            vm((2, 96, 8, 128), BF),
            vm((2, 272, 128), BF),
            vm((4, 4, 4, 272, 128), BF),
            vm((8, 2, 2, 64, 2048), BF),
            vm((4, 8, 128), F32),
            vm((2, 16, 8, 128), F32),
            vm((512, 768), BF),
            vm((4, 8, 128), F32),
            vm((2, 128), F32),
            vm((8, 256), F32),
            dma((6,)),
            dma((2,)), dma((2,)),
            dma((2,)), dma((2,)),
            dma((1,)), dma((2, 6)),
            dma((1,)), dma((4, 3)),
            dma((4,)), dma((2,)),
            dma((2,)), dma((2,)),
            dma((2, 2)), dma((2, 4, 7)),
            dma((1,)), dma((2, 4)),
            dma((1,)), dma((2,)),
            dma((1,)), dma((1,)),
        ],
        compiler_params=pltpu.CompilerParams(
            has_side_effects=True, collective_id=0, vmem_limit_bytes=64 * 1024 * 1024 - 65536
        ),
    )(
        tokens,
        teacher_expert.reshape(1, -1),
        student_expert.reshape(1, -1),
        priority,
        expert_in,
        expert_out,
        teacher_gain.reshape(1, -1),
        student_gain.reshape(1, -1),
        teacher_head,
        student_head,
    )
    return out.reshape(256)


def solution(mesh):
    placed = (
        P("expert", None),
        P("expert", None),
        P("expert", None),
        P("expert", None),
        P("expert", None, "vocab"),
        P("expert", "vocab", None),
        P(),
        P(),
        P(("vocab", "expert"), None),
        P(("vocab", "expert"), None),
    )
    return jax.shard_map(local, mesh=mesh, in_specs=placed, out_specs=P("expert"), check_vma=False)
```
